32 devices in a mesh: wide: 8 (over y, x, core), slab: 4 (over z).
Axes of the slice: x: 2, y: 2, z: 4, core: 2. Of those that a mesh axis runs over, the one named last changes fastest.
Arguments:
- volume: bfloat16 [5, 8, 4096], P(None, 'slab', 'wide'), may hold values from -6 to 6
- back_proj: float32 [8, 4096], P('slab', 'wide'), may hold values from -6 to 6
- dual_state: bfloat16 [5, 8, 16, 1024], P(None, 'slab', 'wide'), may hold values from -6 to 6
- sinogram: bfloat16 [8, 16, 1024], P('slab', 'wide'), may hold values from -6 to 6
- offsets: int32 [8, 16], replicated, may hold values from 0 to 960
- primal_first: bfloat16 [3, 3, 3, 6, 32], replicated, may hold values from -0.5 to 0.5
- primal_second: bfloat16 [3, 3, 3, 32, 32], replicated, may hold values from -0.21875 to 0.21875
- primal_third: bfloat16 [3, 3, 3, 32, 5], replicated, may hold values from -0.21875 to 0.21875
- dual_first: bfloat16 [3, 3, 3, 7, 32], replicated, may hold values from -0.4375 to 0.4375
- dual_second: bfloat16 [3, 3, 3, 32, 32], replicated, may hold values from -0.21875 to 0.21875
- dual_third: bfloat16 [3, 3, 3, 32, 5], replicated, may hold values from -0.21875 to 0.21875
Outputs:
- new_volume: bfloat16 [5, 8, 4096], P(None, 'slab', 'wide')
- new_dual: bfloat16 [5, 8, 16, 1024], P(None, 'slab', 'wide')
- new_back: float32 [8, 4096], P('slab', 'wide')
The draws below stay inside these ranges and needn't reach their ends.
Inputs may be any that keep to these rules, and one draw needn't show every extreme that they name: offsets[t, a] is where tile t's window of 64 bins begins on the detector at angle a.
All inputs are finite; a program needn't handle non-finite values.
Results may differ from the reference program's by a relative error of at most 0.005.
Values may be sent and summed in bfloat16 or wider, within the bound.
A program may use at most 64 MiB of HBM per device.

```python
import math
import jax
import jax.numpy as jnp
from jax import lax

C = 32
MEM = 5
NBINS = 1024
NY = 32
TX = 16
NX = 128
NZ = 8
ANGLES = 16
N_WIDE = 8


def touch_ends(values, key, least, top_value):
    shape = values.shape
    index_at = [jax.random.randint(jax.random.fold_in(key, axis), (), 0, shape[axis]) for axis in range(len(shape))]
    values = values.at[tuple(index_at)].set(least)
    longest = shape.index(max(shape))
    index_at[longest] = (index_at[longest] + 1) % shape[longest]
    return values.at[tuple(index_at)].set(top_value)


def levels(rng, dims, cuts, low, top_value):
    level = 1.0
    for position, parts in cuts:
        draws = jax.random.uniform(jax.random.fold_in(jax.random.fold_in(rng, 6), position), (parts,), jnp.float32, low / len(cuts), top_value / len(cuts))
        level = level * jnp.repeat(jnp.exp(draws), dims[position] // parts).reshape((-1,) + (1,) * (len(dims) - 1 - position))
    return level


def bell_draw(stream_key, extent, scale, limit, split=(), held_as=jnp.bfloat16):
    level = levels(stream_key, extent, split, -0.22, 0.18) if split else 1.0
    entries = jax.random.normal(stream_key, extent, jnp.float32) * scale * level
    return jnp.minimum(jnp.maximum(entries, -limit), limit).astype(held_as)


def setup_inputs(seed: int = 0) -> dict:
    splits = jax.random.split(jax.random.key(seed), 12)
    volume = bell_draw(splits[0], (MEM, NZ, NX * NY), 1.0, 6.0, ((1, 4), (2, 8)))
    back_proj = bell_draw(splits[1], (NZ, NX * NY), 1.0, 6.0, ((0, 4), (1, 8)), jnp.float32)
    dual_state = bell_draw(splits[2], (MEM, NZ, ANGLES, NBINS), 1.0, 6.0, ((1, 4), (2, 8)))
    sinogram = bell_draw(splits[3], (NZ, ANGLES, NBINS), 1.0, 6.0, ((0, 4), (1, 8)))
    offsets = touch_ends(jax.random.randint(splits[4], (N_WIDE, ANGLES), 0, NBINS - NY - 2 * TX + 1), jax.random.fold_in(splits[4], 1), 0, NBINS - NY - 2 * TX).astype(jnp.int32)
    primal_first = bell_draw(splits[5], (3, 3, 3, MEM + 1, C), (27 * (MEM + 1)) ** -0.5, 0.5)
    primal_second = bell_draw(splits[6], (3, 3, 3, C, C), (27 * C) ** -0.5, 0.21875)
    primal_third = bell_draw(splits[7], (3, 3, 3, C, MEM), (27 * C) ** -0.5, 0.21875)
    dual_first = bell_draw(splits[8], (3, 3, 3, MEM + 2, C), (27 * (MEM + 2)) ** -0.5, 0.4375)
    dual_second = bell_draw(splits[9], (3, 3, 3, C, C), (27 * C) ** -0.5, 0.21875)
    dual_third = bell_draw(splits[10], (3, 3, 3, C, MEM), (27 * C) ** -0.5, 0.21875)
    return {"volume": volume, "back_proj": back_proj, "dual_state": dual_state, "sinogram": sinogram, "offsets": offsets, "primal_first": primal_first, "primal_second": primal_second, "primal_third": primal_third, "dual_first": dual_first, "dual_second": dual_second, "dual_third": dual_third}


def make_table(angle_ids, angle_total, rows_x, cols_y):
    window_bins = cols_y + 2 * rows_x
    angle_value = angle_ids.astype(jnp.float32) * (math.pi / angle_total)
    pixels = jnp.arange(rows_x * cols_y, dtype=jnp.int32)
    centre_x = (pixels // cols_y).astype(jnp.float32) - (rows_x - 1) / 2.0
    centre_y = (pixels % cols_y).astype(jnp.float32) - (cols_y - 1) / 2.0
    positions = centre_x[None, :] * jnp.cos(angle_value)[:, None] + centre_y[None, :] * jnp.sin(angle_value)[:, None] + window_bins / 2.0
    detector = jnp.arange(window_bins, dtype=jnp.int32).astype(jnp.float32)
    return jnp.maximum(0.0, 1.0 - jnp.abs(positions[:, :, None] - detector)).astype(jnp.bfloat16)

def convolve(field, weights):
    source = field.astype(jnp.float32)[None]
    kernel = weights.astype(jnp.float32)
    result = lax.conv_general_dilated(source, kernel, (1, 1, 1), ((1, 1), (1, 1), (1, 1)), dimension_numbers=('NCDHW', 'DHWIO', 'NCDHW'), precision=lax.Precision.HIGHEST)
    return result[0]

def reference(volume, back_proj, dual_state, sinogram, offsets, primal_first, primal_second, primal_third, dual_first, dual_second, dual_third):
    grid_view = volume.reshape(MEM, NZ, NX, NY)
    extra_channel = back_proj.astype(jnp.bfloat16).reshape(1, NZ, NX, NY)
    stacked = jnp.concatenate([grid_view, extra_channel], axis=0)
    hidden = jax.nn.relu(convolve(stacked, primal_first)).astype(jnp.bfloat16)
    hidden = jax.nn.relu(convolve(hidden, primal_second)).astype(jnp.bfloat16)
    new_volume = (grid_view.astype(jnp.float32) + convolve(hidden, primal_third)).astype(jnp.bfloat16).reshape(MEM, NZ, NX * NY)
    window_bins = NY + 2 * TX
    pixel_count = TX * NY
    table = make_table(jnp.arange(ANGLES, dtype=jnp.int32), ANGLES, TX, NY).astype(jnp.float32)
    leading = new_volume[0].reshape(NZ, N_WIDE, pixel_count).astype(jnp.float32)
    windows = jnp.einsum('ztp,apj->tazj', leading, table).astype(jnp.bfloat16)
    zero_index = jnp.zeros((), jnp.int32)

    def place_window(window_piece, start_bin):
        return lax.dynamic_update_slice(jnp.zeros((NZ, NBINS), jnp.float32), window_piece.astype(jnp.float32), (zero_index, start_bin))

    def place_tile(tile_id, running):
        spread = jax.vmap(place_window)(windows[tile_id], offsets[tile_id])
        return running + spread
    placed = lax.fori_loop(0, N_WIDE, place_tile, jnp.zeros((ANGLES, NZ, NBINS), jnp.float32))
    projected = (placed * (1.0 / math.sqrt(NY))).transpose(1, 0, 2).astype(jnp.bfloat16)
    dual_in = jnp.concatenate([dual_state, projected[None], sinogram[None]], axis=0)
    hidden = jax.nn.relu(convolve(dual_in, dual_first)).astype(jnp.bfloat16)
    hidden = jax.nn.relu(convolve(hidden, dual_second)).astype(jnp.bfloat16)
    new_dual = (dual_state.astype(jnp.float32) + convolve(hidden, dual_third)).astype(jnp.bfloat16)
    by_angle = new_dual[0].transpose(1, 0, 2)

    def cut_window(plane, start_bin):
        return lax.dynamic_slice(plane, (zero_index, start_bin), (NZ, window_bins))

    def back_tile(tile_id):
        pieces = jax.vmap(cut_window)(by_angle, offsets[tile_id])
        return jnp.einsum('azj,apj->zp', pieces.astype(jnp.float32), table)
    per_tile = lax.map(back_tile, jnp.arange(N_WIDE, dtype=jnp.int32))
    new_back = per_tile.transpose(1, 0, 2).reshape(NZ, NX * NY) * (1.0 / math.sqrt(ANGLES))
    return (new_volume, new_dual, new_back)
```

```python
import functools
import math

import jax
import jax.numpy as jnp
import numpy as np
from jax import lax
from jax.experimental import pallas as pl
from jax.experimental.pallas import tpu as pltpu
from jax.sharding import PartitionSpec as P

NY = 32
TX = 16
HALO = 3
CH = 8
MESH = pl.DeviceIdType.MESH
F32 = jnp.float32
BF16 = jnp.bfloat16
VMEM_LIMIT = 60 * 1024 * 1024


def trig_rows(angle_total):
    window = NY + 2 * TX
    angle = np.arange(angle_total, dtype=np.float32) * np.float32(math.pi / angle_total)
    rows = np.zeros((8, angle_total * window), np.float32)
    rows[0] = np.repeat(np.cos(angle), window)
    rows[1] = np.repeat(np.sin(angle), window)
    rows[2] = np.tile(np.arange(window, dtype=np.float32), angle_total)
    return rows


def build_table(trig, table):
    cosine, sine, detector = trig[0:1, :], trig[1:2, :], trig[2:3, :]
    centre_y = lax.broadcasted_iota(jnp.int32, (NY, trig.shape[1]), 0).astype(F32) - (NY - 1) / 2.0

    def row(i, carry):
        centre_x = lax.convert_element_type(i, F32) - (TX - 1) / 2.0
        positions = centre_x * cosine + centre_y * sine + (NY + 2 * TX) / 2.0
        value = jnp.maximum(0.0, 1.0 - jnp.abs(positions - detector))
        table[pl.ds(pl.multiple_of(i * NY, NY), NY), :] = value.astype(BF16)
        return carry

    lax.fori_loop(0, TX, row, 0)


def build_band(weights, stage, out, out_slices, same, c_pad, bin_pad, o_pad, turn=False):
    if turn:
        c_out, _, c_in = weights.shape[2:]
    else:
        c_in, c_out = weights.shape[3:]
    block = bin_pad * c_pad
    in_slices = out_slices if same else out_slices + 2
    chunk = in_slices * block
    width = chunk if chunk % 128 == 0 else -(-3 * chunk // 128) * 128
    held = -(-3 * block // 128) * 128
    pieces = []
    for d1 in range(3):
        if turn:
            lines = []
            for d0 in range(3):
                lines += [weights[d0, d1, :, d2, :].astype(F32) for d2 in range(3)]
            flat = jnp.concatenate(lines + [jnp.zeros((c_out, held - 9 * c_in), F32)], axis=1)
            flat = jnp.concatenate([flat, jnp.zeros((o_pad - c_out, held), F32)], axis=0)
        else:
            stage[...] = jnp.zeros_like(stage)
            for d0 in range(3):
                for d2 in range(3):
                    at = (d0 * bin_pad + d2) * c_pad
                    stage[at : at + c_in, :c_out] = weights[d0, d1, d2].astype(F32)
            flat = stage[:held, :].T[:o_pad]
        if width > held:
            flat = jnp.concatenate([flat, jnp.zeros((o_pad, width - held), F32)], axis=1)
        pieces.append(flat[:, :width])
    lane = lax.broadcasted_iota(jnp.int32, (1, width), 1)

    def turned(piece, by):
        by = by % width
        return pltpu.roll(piece, by, axis=1) if by else piece

    waiting = []
    for z in range(out_slices):
        if chunk % 128 == 0:
            parts = []
            for piece in pieces:
                part = turned(piece, (z - 1 if same else z) * block)
                if same and z == 0:
                    part = jnp.where(lane < 2 * block, part, 0.0)
                if same and z == out_slices - 1:
                    part = jnp.where(lane >= (z - 1) * block, part, 0.0)
                parts.append(part)
            row = jnp.concatenate(parts, axis=1)
        else:
            assert not same
            row = sum(turned(piece, d1 * chunk + z * block) for d1, piece in enumerate(pieces))
        waiting.append(row)
        rows = len(waiting) * o_pad
        if rows % 16 == 0:
            both = waiting[0] if len(waiting) == 1 else jnp.concatenate(waiting, axis=0)
            out[(z + 1) * o_pad - rows : (z + 1) * o_pad, :] = both[:, : 3 * chunk].astype(BF16)
            waiting = []
    assert not waiting


def shifted(value, by):
    lanes = value.shape[-1]
    return value if by == 0 else pltpu.roll(value, (-by) % lanes, axis=value.ndim - 1)


def spans(block):
    reach = -(-HALO // block)
    result = {}
    for d in range(-reach, reach + 1):
        count = block if d == 0 else min(block, HALO - (abs(d) - 1) * block)
        first = block - count if d > 0 else 0
        result[d] = (first, count, first - d * block + HALO)
    return reach, result


def whole_kernel(
    wide, slab, *refs
):
    given = refs[:12]
    vol_out, dual_out, back_out = refs[12:15]
    held, in_sem = refs[15:27], refs[27]
    volume, back_proj, dual_state, sinogram, offsets, p1, p2, p3, d1_w, d2_w, d3_w, trig = held
    (
    psrc, dsrc, frame, dual_in, arrived, wsend, table, stage, pw1, pw2, pw3, dw1, dw2, dw3,
    px1, px2, nv, chosen, proj, x1, x2, x3, nd, cut, pieces, returned,
    p_send, p_recv, d_send, d_recv, a_send, a_recv, b_send, b_recv,
    ) = refs[28:]
    w = lax.axis_index("wide")
    s = lax.axis_index("slab")
    mem, slices, pixels = volume.shape
    angles, bins = dual_state.shape[2:]
    angle_total = angles * wide
    depth = slices * slab
    edge = 4 * NY
    lanes = pixels + 2 * edge
    window = NY + 2 * TX
    hidden_channels = p1.shape[4]
    wide_angles = angles + 2 * HALO
    deep = slices + 2 * HALO
    reach_a, span_a = spans(angles)
    reach_z, span_z = spans(slices)
    group = angles * window
    cover = (2 * reach_a + 1) * group

    def inside(i, j):
        return (i >= 0) & (i < wide) & (j >= 0) & (j < slab)

    frame[...] = jnp.zeros_like(frame)
    dual_in[...] = jnp.zeros_like(dual_in)

    reach_w = max(1, reach_a)
    greet = [
        (i, j) for i in range(-reach_w, reach_w + 1) for j in range(-(slab - 1), slab) if (i, j) != (0, 0)
    ]
    barrier = pltpu.get_barrier_semaphore()
    total = jnp.int32(wide - 1)
    for i, j in greet:
        there = inside(w + i, s + j)

        @pl.when(there)
        def _():
            pl.semaphore_signal(barrier, inc=1, device_id=(w + i, s + j), device_id_type=MESH)

        total = total + jnp.where(there, 1, 0)
    for k in range(1, wide):
        pl.semaphore_signal(barrier, inc=1, device_id=(lax.rem(w + k, wide), s), device_id_type=MESH)

    loads = [pltpu.make_async_copy(src, dst, in_sem.at[n]) for n, (src, dst) in enumerate(zip(given, held))]
    for load in loads:
        load.start()
    wsend[...] = jnp.zeros_like(wsend)
    for load in loads[:4]:
        load.wait()
    for z in range(slices):
        lines = [volume[c].astype(F32)[z : z + 1] for c in range(mem)]
        lines += [back_proj[z : z + 1, :], jnp.zeros((CH - mem - 1, pixels), F32)]
        psrc[z] = jnp.concatenate(lines, axis=0).astype(BF16)
        for a in range(angles):
            lines = [dual_state[c, z].astype(F32)[a : a + 1] for c in range(mem)]
            lines += [jnp.zeros((1, bins), F32), sinogram[z].astype(F32)[a : a + 1]]
            lines += [jnp.zeros((CH - mem - 2, bins), F32)]
            dsrc[a, z] = jnp.concatenate(lines, axis=0).astype(BF16)
    frame[pl.ds(s * slices, slices), :, edge : edge + pixels] = psrc[...]
    dual_in[HALO : HALO + angles, HALO : HALO + slices] = dsrc[...]
    pl.semaphore_wait(barrier, total)

    def p_copy(i, j, row, target):
        if i == 0:
            src, dst = pl.ds(0, pixels), pl.ds(edge, pixels)
        elif i > 0:
            src, dst = pl.ds(pixels - edge, edge), pl.ds(0, edge)
        else:
            src, dst = pl.ds(0, edge), pl.ds(edge + pixels, edge)
        return pltpu.make_async_remote_copy(
            src_ref=psrc.at[:, :, src],
            dst_ref=frame.at[pl.ds(row * slices, slices), :, dst],
            send_sem=p_send.at[i + 1, j + slab - 1],
            recv_sem=p_recv.at[i + 1, j + slab - 1],
            device_id=target,
            device_id_type=MESH,
        )

    def d_copy(i, j, target):
        a0, an, ad = span_a[i]
        z0, zn, zd = span_z[j]
        return pltpu.make_async_remote_copy(
            src_ref=dsrc.at[pl.ds(a0, an), pl.ds(z0, zn)],
            dst_ref=dual_in.at[pl.ds(ad, an), pl.ds(zd, zn)],
            send_sem=d_send.at[i + reach_a, j + reach_z],
            recv_sem=d_recv.at[i + reach_a, j + reach_z],
            device_id=target,
            device_id_type=MESH,
        )

    p_moves = [(i, j) for i in (-1, 0, 1) for j in range(-(slab - 1), slab) if (i, j) != (0, 0)]
    d_moves = [(i, j) for i in span_a for j in span_z if (i, j) != (0, 0)]
    for i, j in p_moves:

        @pl.when(inside(w + i, s + j))
        def _():
            p_copy(i, j, s, (w + i, s + j)).start()

    for i, j in d_moves:

        @pl.when(inside(w + i, s + j))
        def _():
            d_copy(i, j, (w + i, s + j)).start()


    for load in loads[4:]:
        load.wait()
    batch = math.gcd(wide, 8)
    groups = wide // batch
    relative = lax.broadcasted_iota(jnp.int32, (window, bins), 1) - lax.broadcasted_iota(
        jnp.int32, (window, bins), 0
    )

    def select(a, g):
        column = jnp.clip(w * angles + a - HALO, 0, angle_total - 1)
        rows = offsets[pl.ds(g * batch, batch), :]
        here = lax.broadcasted_iota(jnp.int32, rows.shape, 1) == column
        begin = jnp.sum(jnp.where(here, rows, 0), axis=1, keepdims=True)
        for t in range(batch):
            hit = relative == begin[t : t + 1]
            chosen[a, t * window : (t + 1) * window, :] = jnp.where(hit, 1.0, 0.0).astype(BF16)

    build_band(p1, stage, pw1, depth, True, CH, 4, hidden_channels)
    build_band(p2, stage, pw2, depth, True, hidden_channels, 3, hidden_channels)
    build_band(p3, stage, pw3, depth, True, hidden_channels, 3, CH, True)
    build_table(trig, table)
    build_band(d1_w, stage, dw1, deep - 2, False, CH, 4, hidden_channels)
    build_band(d2_w, stage, dw2, deep - 4, False, hidden_channels, 3, hidden_channels)
    build_band(d3_w, stage, dw3, deep - 6, False, hidden_channels, 3, CH, True)
    if groups == 1:
        for a in range(wide_angles):
            select(a, 0)

    for i, j in p_moves:

        @pl.when(inside(w - i, s - j))
        def _():
            p_copy(i, j, s - j, (w, s)).wait_recv()


    plane = lax.broadcasted_iota(jnp.int32, (1, lanes), 1)
    y = plane % NY
    x = w * TX + plane // NY - 4
    grid_mask = (x >= 0) & (x < wide * TX)
    y_mask = {-1: y > 0, 0: None, 1: y < NY - 1}

    def tap(value, d1, d2):
        moved = shifted(value, NY * d1 + d2)
        return moved if d2 == 0 else jnp.where(y_mask[d2], moved, 0.0)

    field = frame[...].astype(F32)
    pblank = jnp.zeros((CH, lanes), F32)
    for z in range(depth):
        for d1 in range(3):
            parts = [tap(field[z], d1 - 1, d2) for d2 in (-1, 0, 1)] + [pblank]
            px1[pl.ds((d1 * depth + z) * 4 * CH, 4 * CH), :] = jnp.concatenate(parts, axis=0).astype(BF16)

    def spread(hidden):
        hid = hidden.shape[0] // depth
        for d1 in range(3):
            for d2 in range(3):
                moved = tap(hidden, d1 - 1, d2 - 1).astype(BF16)
                for z in range(depth):
                    px2[pl.ds(((d1 * depth + z) * 3 + d2) * hid, hid), :] = moved[z * hid : (z + 1) * hid]

    one = jnp.dot(pw1[...], px1[...], preferred_element_type=F32)
    spread(jnp.where(grid_mask, jnp.maximum(one, 0.0), 0.0))
    two = jnp.dot(pw2[...], px2[...], preferred_element_type=F32)
    spread(jnp.where(grid_mask, jnp.maximum(two, 0.0), 0.0))
    three = jnp.dot(pw3[...], px2[...], preferred_element_type=F32)
    updated = field.reshape(depth * CH, lanes) + three
    updated = updated[:, edge : edge + pixels].astype(BF16).astype(F32)
    nv[...] = updated.reshape(depth, CH, pixels)
    leading = jnp.concatenate([updated[z * CH : z * CH + 1] for z in range(depth)], axis=0).astype(BF16)
    windows = jnp.dot(leading, table[...], preferred_element_type=F32).astype(BF16)
    wsend[:, reach_a * group : (reach_a + wide) * group] = windows

    def a_copy(k, row, target):
        lanes_of = pl.ds(pl.multiple_of(target * group, 128), cover)
        return pltpu.make_async_remote_copy(
            src_ref=wsend.at[:, lanes_of],
            dst_ref=arrived.at[row],
            send_sem=a_send.at[k - 1],
            recv_sem=a_recv.at[k - 1],
            device_id=(target, s),
            device_id_type=MESH,
        )

    for k in range(1, wide):
        a_copy(k, w, lax.rem(w + k, wide)).start()
    arrived[w] = wsend[:, pl.ds(pl.multiple_of(w * group, 128), cover)]

    mine = [nv[s * slices + z] for z in range(slices)]
    for c in range(mem):
        vol_out[c] = jnp.concatenate([m[c : c + 1] for m in mine], axis=0).astype(BF16)
    proj[...] = jnp.zeros_like(proj)
    cut[...] = jnp.zeros_like(cut)
    for i, j in d_moves:

        @pl.when(inside(w - i, s - j))
        def _():
            d_copy(i, j, (w, s)).wait_recv()

    for k in range(1, wide):
        a_copy(k, lax.rem(w + wide - k, wide), w).wait_recv()

    for a in range(wide_angles):
        at = (a - HALO + reach_a * angles) * window

        def place(g, carry):
            if groups > 1:
                select(a, g)
            halves = [arrived[g * batch + t].astype(F32)[:, at : at + window] for t in range(batch)]
            return carry + jnp.dot(
                jnp.concatenate(halves, axis=1).astype(BF16), chosen[a], preferred_element_type=F32
            )

        placed = jnp.zeros((depth, bins), F32)
        placed = place(0, placed) if groups == 1 else lax.fori_loop(0, groups, place, placed)
        scaled = (placed * (1.0 / math.sqrt(NY))).astype(BF16).astype(F32)
        for z in range(depth):
            proj[HALO + z, a : a + 1, :] = scaled[z : z + 1]

    lane = lax.broadcasted_iota(jnp.int32, (1, bins), 1)
    row8 = lax.broadcasted_iota(jnp.int32, (CH, bins), 0)
    low, high = lane > 0, lane < bins - 1
    blank = jnp.zeros((CH, bins), F32)

    def three(value):
        return (
            jnp.where(low, shifted(value, -1), 0.0),
            value,
            jnp.where(high, shifted(value, 1), 0.0),
        )

    for a in range(wide_angles):
        for z in range(deep):
            line = proj[s * slices + z, a : a + 1, :]
            value = jnp.where(row8 == 5, line, dual_in[a, z].astype(F32))
            left, mid, right = three(value)
            x1[pl.ds((a * deep + z) * 4 * CH, 4 * CH), :] = jnp.concatenate(
                [left, mid, right, blank], axis=0
            ).astype(BF16)

    def layer(weight, source, dest, out_angles, in_slices, per_slice, margin):
        out_slices = in_slices - 2
        hid = weight.shape[0] // out_slices
        rows = in_slices * per_slice
        row_z = s * slices - margin + lax.broadcasted_iota(jnp.int32, (hid * out_slices, 1), 0) // hid
        z_ok = (row_z >= 0) & (row_z < depth)
        for a in range(out_angles):
            angle = w * angles - margin + a
            ok = z_ok & (angle >= 0) & (angle < angle_total)
            value = jnp.dot(weight[...], source[pl.ds(a * rows, 3 * rows), :], preferred_element_type=F32)
            value = jnp.where(ok, jnp.maximum(value, 0.0), 0.0)
            for d2, moved in enumerate(three(value)):
                moved = moved.astype(BF16)
                for z in range(out_slices):
                    dest[pl.ds(((a * out_slices + z) * 3 + d2) * hid, hid), :] = moved[z * hid : (z + 1) * hid]

    hidden = dw2.shape[0] // (deep - 4)
    layer(dw1, x1, x2, wide_angles - 2, deep, 4 * CH, 2)
    layer(dw2, x2, x3, wide_angles - 4, deep - 2, 3 * hidden, 1)
    rows = (deep - 4) * 3 * hidden
    for a in range(angles):
        value = jnp.dot(dw3[...], x3[pl.ds(a * rows, 3 * rows), :], preferred_element_type=F32)
        own = dual_in[HALO + a, HALO : HALO + slices].astype(F32).reshape(slices * CH, bins)
        value = (own + value).astype(BF16).astype(F32)
        nd[a] = value
        for z in range(slices):
            cut[a, z : z + 1, :] = value[z * CH : z * CH + 1]

    def take(g, carry):
        found = []
        for a in range(angles):
            if groups > 1:
                select(HALO + a, g)
            found.append(
                lax.dot_general(
                    cut[a].astype(BF16), chosen[HALO + a], (((1,), (1,)), ((), ())), preferred_element_type=F32
                )
            )
        for t in range(batch):
            pieces[g * batch + t] = jnp.concatenate(
                [f[:, t * window : (t + 1) * window] for f in found], axis=1
            )
        return carry

    if groups == 1:
        take(0, 0)
    else:
        lax.fori_loop(0, groups, take, 0)

    def b_copy(k, row, target):
        return pltpu.make_async_remote_copy(
            src_ref=pieces.at[target],
            dst_ref=returned.at[row],
            send_sem=b_send.at[k - 1],
            recv_sem=b_recv.at[k - 1],
            device_id=(target, s),
            device_id_type=MESH,
        )

    for k in range(1, wide):
        b_copy(k, w, lax.rem(w + k, wide)).start()
    returned[w] = pieces[w]
    for z in range(slices):
        for c in range(mem):
            lines = [nd[a, z * CH + c : z * CH + c + 1, :] for a in range(angles)]
            dual_out[c, z] = jnp.concatenate(lines, axis=0).astype(BF16)
    for k in range(1, wide):
        b_copy(k, lax.rem(w + wide - k, wide), w).wait_recv()
    lines = jnp.concatenate([returned[t] for t in range(wide)], axis=1).astype(BF16)
    summed = lax.dot_general(lines, table[...], (((1,), (1,)), ((), ())), preferred_element_type=F32)
    back_out[...] = summed[:slices] * (1.0 / math.sqrt(angle_total))
    for k in range(1, wide):
        b_copy(k, w, lax.rem(w + k, wide)).wait_send()
    for i, j in p_moves:

        @pl.when(inside(w + i, s + j))
        def _():
            p_copy(i, j, s, (w, s)).wait_send()

    for i, j in d_moves:

        @pl.when(inside(w + i, s + j))
        def _():
            d_copy(i, j, (w, s)).wait_send()

    for k in range(1, wide):
        a_copy(k, w, lax.rem(w + k, wide)).wait_send()


def hand_on(outs):
    def kernel(*refs):
        for src, dst in zip(refs[:3], refs[3:]):
            dst[...] = src[...]

    space = pl.BlockSpec(memory_space=pltpu.VMEM)
    return pl.pallas_call(
        kernel,
        out_shape=tuple(jax.ShapeDtypeStruct(o.shape, o.dtype) for o in outs),
        in_specs=[space] * 3,
        out_specs=(space,) * 3,
        name="hand_on",
    )(*outs)


def body(wide, slab, volume, back_proj, dual_state, sinogram, offsets, p1, p2, p3, d1, d2, d3):
    mem, slices, pixels = volume.shape
    angles, bins = dual_state.shape[2:]
    depth = slices * slab
    angle_total = angles * wide
    hidden = p1.shape[4]
    group = angles * (NY + 2 * TX)
    reach_a, _ = spans(angles)
    reach_z, _ = spans(slices)
    lanes = pixels + 8 * NY
    wide_angles = angles + 2 * HALO
    deep = slices + 2 * HALO
    dma = pltpu.SemaphoreType.DMA
    vmem = pltpu.VMEM
    space = pl.BlockSpec(memory_space=pltpu.VMEM)
    args = (volume, back_proj, dual_state, sinogram, offsets, p1, p2, p3.transpose(0, 1, 4, 2, 3))
    args += (d1, d2, d3.transpose(0, 1, 4, 2, 3), jnp.asarray(trig_rows(angle_total)))
    outs = pl.pallas_call(
        functools.partial(whole_kernel, wide, slab),
        out_shape=(
            jax.ShapeDtypeStruct(volume.shape, BF16),
            jax.ShapeDtypeStruct(dual_state.shape, BF16),
            jax.ShapeDtypeStruct(back_proj.shape, F32),
        ),
        in_specs=[pl.BlockSpec(memory_space=pl.ANY)] * 12,
        out_specs=(space,) * 3,
        scratch_shapes=[vmem(a.shape, a.dtype) for a in args]
        + [dma((12,))]
        + [
            vmem((slices, CH, pixels), BF16),
            vmem((angles, slices, CH, bins), BF16),
            vmem((depth, CH, lanes), BF16),
            vmem((wide_angles, deep, CH, bins), BF16),
            vmem((wide, depth, (2 * reach_a + 1) * group), BF16),
            vmem((depth, (wide + 2 * reach_a) * group), BF16),
            vmem((pixels, angle_total * (NY + 2 * TX)), BF16),
            vmem((-(-9 * hidden // 128) * 128, 128), F32),
            vmem((depth * hidden, 12 * depth * CH), BF16),
            vmem((depth * hidden, 9 * depth * hidden), BF16),
            vmem((depth * CH, 9 * depth * hidden), BF16),
            vmem(((deep - 2) * hidden, 12 * deep * CH), BF16),
            vmem(((deep - 4) * hidden, 9 * (deep - 2) * hidden), BF16),
            vmem(((deep - 6) * CH, 9 * (deep - 4) * hidden), BF16),
            vmem((12 * depth * CH, lanes), BF16),
            vmem((9 * depth * hidden, lanes), BF16),
            vmem((depth, CH, pixels), F32),
            vmem((wide_angles, math.gcd(wide, 8) * (NY + 2 * TX), bins), BF16),
            vmem((depth + 2 * HALO, wide_angles, bins), F32),
            vmem((wide_angles * deep * 4 * CH, bins), BF16),
            vmem(((wide_angles - 2) * (deep - 2) * 3 * hidden, bins), BF16),
            vmem(((wide_angles - 4) * (deep - 4) * 3 * hidden, bins), BF16),
            vmem((angles, slices * CH, bins), F32),
            vmem((angles, 8, bins), F32),
            vmem((wide, 8, group), F32),
            vmem((wide, 8, group), F32),
            dma((3, 2 * slab - 1)),
            dma((3, 2 * slab - 1)),
            dma((2 * reach_a + 1, 2 * reach_z + 1)),
            dma((2 * reach_a + 1, 2 * reach_z + 1)),
            dma((wide - 1,)),
            dma((wide - 1,)),
            dma((wide - 1,)),
            dma((wide - 1,)),
        ],
        compiler_params=pltpu.CompilerParams(
            collective_id=0, has_side_effects=True, vmem_limit_bytes=VMEM_LIMIT
        ),
        name="whole_kernel",
    )(*args)
    return hand_on(outs)


def solution(mesh):
    wide, slab = mesh.shape["wide"], mesh.shape["slab"]
    in_specs = (
        P(None, "slab", "wide"),
        P("slab", "wide"),
        P(None, "slab", "wide", None),
        P("slab", "wide", None),
    ) + (P(),) * 7
    out_specs = (P(None, "slab", "wide"), P(None, "slab", "wide", None), P("slab", "wide"))
    return jax.shard_map(
        functools.partial(body, wide, slab), mesh=mesh, in_specs=in_specs, out_specs=out_specs, check_vma=False
    )
```

```python
import functools
import math

import jax
import jax.numpy as jnp
import numpy as np
from jax import lax
from jax.experimental import pallas as pl
from jax.experimental.pallas import tpu as pltpu
from jax.sharding import PartitionSpec as P

NY = 32
TX = 16
HALO = 3
CH = 8
MARGIN = 4
MESH = pl.DeviceIdType.MESH
F32 = jnp.float32
BF16 = jnp.bfloat16
VMEM_LIMIT = 60 * 1024 * 1024


def trig_rows(angle_total):
    window = NY + 2 * TX
    angle = np.arange(angle_total, dtype=np.float32) * np.float32(math.pi / angle_total)
    rows = np.zeros((8, angle_total * window), np.float32)
    rows[0] = np.repeat(np.cos(angle), window)
    rows[1] = np.repeat(np.sin(angle), window)
    rows[2] = np.tile(np.arange(window, dtype=np.float32), angle_total)
    return rows


def build_table(trig, table, detector=None):
    cosine, sine = trig[0:1, :], trig[1:2, :]
    detector = trig[2:3, :] if detector is None else detector
    centre_y = lax.broadcasted_iota(jnp.int32, (NY, trig.shape[1]), 0).astype(F32) - (NY - 1) / 2.0

    def row(i, carry):
        centre_x = lax.convert_element_type(i, F32) - (TX - 1) / 2.0
        positions = centre_x * cosine + centre_y * sine + (NY + 2 * TX) / 2.0
        value = jnp.maximum(0.0, 1.0 - jnp.abs(positions - detector))
        table[pl.ds(pl.multiple_of(i * NY, NY), NY), :] = value.astype(BF16)
        return carry

    lax.fori_loop(0, TX, row, 0)


def build_band(weights, stage, out, out_slices, same, c_pad, bin_pad, o_pad, turn=False):
    if turn:
        c_out, _, c_in = weights.shape[2:]
    else:
        c_in, c_out = weights.shape[3:]
    block = bin_pad * c_pad
    in_slices = out_slices if same else out_slices + 2
    chunk = in_slices * block
    width = chunk if chunk % 128 == 0 else -(-3 * chunk // 128) * 128
    held = -(-3 * block // 128) * 128
    pieces = []
    for d1 in range(3):
        if turn:
            lines = []
            for d0 in range(3):
                lines += [weights[d0, d1, :, d2, :].astype(F32) for d2 in range(3)]
            flat = jnp.concatenate(lines + [jnp.zeros((c_out, held - 9 * c_in), F32)], axis=1)
            flat = jnp.concatenate([flat, jnp.zeros((o_pad - c_out, held), F32)], axis=0)
        else:
            stage[...] = jnp.zeros_like(stage)
            for d0 in range(3):
                for d2 in range(3):
                    at = (d0 * bin_pad + d2) * c_pad
                    stage[at : at + c_in, :c_out] = weights[d0, d1, d2].astype(F32)
            flat = stage[:held, :].T[:o_pad]
        if width > held:
            flat = jnp.concatenate([flat, jnp.zeros((o_pad, width - held), F32)], axis=1)
        pieces.append(flat[:, :width])
    lane = lax.broadcasted_iota(jnp.int32, (1, width), 1)

    def turned(piece, by):
        by = by % width
        return pltpu.roll(piece, by, axis=1) if by else piece

    waiting = []
    for z in range(out_slices):
        if chunk % 128 == 0:
            parts = []
            for piece in pieces:
                part = turned(piece, (z - 1 if same else z) * block)
                if same and z == 0:
                    part = jnp.where(lane < 2 * block, part, 0.0)
                if same and z == out_slices - 1:
                    part = jnp.where(lane >= (z - 1) * block, part, 0.0)
                parts.append(part)
            row = jnp.concatenate(parts, axis=1)
        else:
            assert not same
            row = sum(turned(piece, d1 * chunk + z * block) for d1, piece in enumerate(pieces))
        waiting.append(row)
        rows = len(waiting) * o_pad
        if rows % 16 == 0:
            both = waiting[0] if len(waiting) == 1 else jnp.concatenate(waiting, axis=0)
            out[(z + 1) * o_pad - rows : (z + 1) * o_pad, :] = both[:, : 3 * chunk].astype(BF16)
            waiting = []
    assert not waiting


def shifted(value, by):
    lanes = value.shape[-1]
    return value if by == 0 else pltpu.roll(value, (-by) % lanes, axis=value.ndim - 1)


def spans(block):
    reach = -(-HALO // block)
    result = {}
    for d in range(-reach, reach + 1):
        count = block if d == 0 else min(block, HALO - (abs(d) - 1) * block)
        first = block - count if d > 0 else 0
        result[d] = (first, count, first - d * block + HALO)
    return reach, result


def whole_kernel(
    wide, slab, *refs
):
    given = refs[:12]
    vol_out, dual_out, back_out = refs[12:15]
    held, in_sem = refs[15:27], refs[27]
    volume, back_proj, dual_state, sinogram, offsets, p1, p2, p3, d1_w, d2_w, d3_w, trig = held
    (
    psrc, dsrc, frame, dual_in, arrived, wsend, table, stage, pw1, pw2, pw3, dw1, dw2, dw3,
    px1, px2, nv, chosen, proj, x1, x2, x3, nd, cut, pieces, returned,
    p_send, p_recv, d_send, d_recv, a_send, a_recv, b_send, b_recv,
    ) = refs[28:]
    w = lax.axis_index("wide")
    s = lax.axis_index("slab")
    mem, slices, pixels = volume.shape
    angles, bins = dual_state.shape[2:]
    angle_total = angles * wide
    depth = slices * slab
    edge = 4 * NY
    lanes = pixels + 2 * edge
    window = NY + 2 * TX
    hidden_channels = p1.shape[4]
    wide_angles = angles + 2 * HALO
    deep = slices + 2 * HALO
    reach_a, span_a = spans(angles)
    reach_z, span_z = spans(slices)
    group = angles * window
    cover = (2 * reach_a + 1) * group

    def inside(i, j):
        return (i >= 0) & (i < wide) & (j >= 0) & (j < slab)

    frame[...] = jnp.zeros_like(frame)
    dual_in[...] = jnp.zeros_like(dual_in)

    reach_w = max(1, reach_a)
    greet = [
        (i, j) for i in range(-reach_w, reach_w + 1) for j in range(-(slab - 1), slab) if (i, j) != (0, 0)
    ]
    barrier = pltpu.get_barrier_semaphore()
    total = jnp.int32(wide - 1)
    for i, j in greet:
        there = inside(w + i, s + j)

        @pl.when(there)
        def _():
            pl.semaphore_signal(barrier, inc=1, device_id=(w + i, s + j), device_id_type=MESH)

        total = total + jnp.where(there, 1, 0)
    for k in range(1, wide):
        pl.semaphore_signal(barrier, inc=1, device_id=(lax.rem(w + k, wide), s), device_id_type=MESH)

    loads = [pltpu.make_async_copy(src, dst, in_sem.at[n]) for n, (src, dst) in enumerate(zip(given, held))]
    for load in loads:
        load.start()
    wsend[...] = jnp.zeros_like(wsend)
    for load in loads[:4]:
        load.wait()
    for z in range(slices):
        lines = [volume[c].astype(F32)[z : z + 1] for c in range(mem)]
        lines += [back_proj[z : z + 1, :], jnp.zeros((CH - mem - 1, pixels), F32)]
        psrc[z] = jnp.concatenate(lines, axis=0).astype(BF16)
        for a in range(angles):
            lines = [dual_state[c, z].astype(F32)[a : a + 1] for c in range(mem)]
            lines += [jnp.zeros((1, bins), F32), sinogram[z].astype(F32)[a : a + 1]]
            lines += [jnp.zeros((CH - mem - 2, bins), F32)]
            dsrc[a, z] = jnp.concatenate(lines, axis=0).astype(BF16)
    frame[pl.ds(s * slices, slices), :, edge : edge + pixels] = psrc[...]
    dual_in[HALO : HALO + angles, HALO : HALO + slices] = dsrc[...]
    pl.semaphore_wait(barrier, total)

    def p_copy(i, j, row, target):
        if i == 0:
            src, dst = pl.ds(0, pixels), pl.ds(edge, pixels)
        elif i > 0:
            src, dst = pl.ds(pixels - edge, edge), pl.ds(0, edge)
        else:
            src, dst = pl.ds(0, edge), pl.ds(edge + pixels, edge)
        return pltpu.make_async_remote_copy(
            src_ref=psrc.at[:, :, src],
            dst_ref=frame.at[pl.ds(row * slices, slices), :, dst],
            send_sem=p_send.at[i + 1, j + slab - 1],
            recv_sem=p_recv.at[i + 1, j + slab - 1],
            device_id=target,
            device_id_type=MESH,
        )

    def d_copy(i, j, target):
        a0, an, ad = span_a[i]
        z0, zn, zd = span_z[j]
        return pltpu.make_async_remote_copy(
            src_ref=dsrc.at[pl.ds(a0, an), pl.ds(z0, zn)],
            dst_ref=dual_in.at[pl.ds(ad, an), pl.ds(zd, zn)],
            send_sem=d_send.at[i + reach_a, j + reach_z],
            recv_sem=d_recv.at[i + reach_a, j + reach_z],
            device_id=target,
            device_id_type=MESH,
        )

    p_moves = [(i, j) for i in (-1, 0, 1) for j in range(-(slab - 1), slab) if (i, j) != (0, 0)]
    d_moves = [(i, j) for i in span_a for j in span_z if (i, j) != (0, 0)]
    for i, j in p_moves:

        @pl.when(inside(w + i, s + j))
        def _():
            p_copy(i, j, s, (w + i, s + j)).start()

    for i, j in d_moves:

        @pl.when(inside(w + i, s + j))
        def _():
            d_copy(i, j, (w + i, s + j)).start()


    for load in loads[4:]:
        load.wait()
    batch = math.gcd(wide, 8)
    groups = wide // batch
    relative = lax.broadcasted_iota(jnp.int32, (window, bins), 1) - lax.broadcasted_iota(
        jnp.int32, (window, bins), 0
    )

    def select(a, g):
        column = jnp.clip(w * angles + a - HALO, 0, angle_total - 1)
        rows = offsets[pl.ds(g * batch, batch), :]
        here = lax.broadcasted_iota(jnp.int32, rows.shape, 1) == column
        begin = jnp.sum(jnp.where(here, rows, 0), axis=1, keepdims=True)
        for t in range(batch):
            hit = relative == begin[t : t + 1]
            chosen[a, t * window : (t + 1) * window, :] = jnp.where(hit, 1.0, 0.0).astype(BF16)

    build_band(p1, stage, pw1, depth, True, CH, 4, hidden_channels)
    build_band(p2, stage, pw2, depth, True, hidden_channels, 3, hidden_channels)
    build_band(p3, stage, pw3, depth, True, hidden_channels, 3, CH, True)
    build_table(trig, table)
    build_band(d1_w, stage, dw1, deep - 2, False, CH, 4, hidden_channels)
    build_band(d2_w, stage, dw2, deep - 4, False, hidden_channels, 3, hidden_channels)
    build_band(d3_w, stage, dw3, deep - 6, False, hidden_channels, 3, CH, True)
    if groups == 1:
        for a in range(wide_angles):
            select(a, 0)

    for i, j in p_moves:

        @pl.when(inside(w - i, s - j))
        def _():
            p_copy(i, j, s - j, (w, s)).wait_recv()


    plane = lax.broadcasted_iota(jnp.int32, (1, lanes), 1)
    y = plane % NY
    x = w * TX + plane // NY - 4
    grid_mask = (x >= 0) & (x < wide * TX)
    y_mask = {-1: y > 0, 0: None, 1: y < NY - 1}

    def tap(value, d1, d2):
        moved = shifted(value, NY * d1 + d2)
        return moved if d2 == 0 else jnp.where(y_mask[d2], moved, 0.0)

    field = frame[...].astype(F32)
    pblank = jnp.zeros((CH, lanes), F32)
    for z in range(depth):
        for d1 in range(3):
            parts = [tap(field[z], d1 - 1, d2) for d2 in (-1, 0, 1)] + [pblank]
            px1[pl.ds((d1 * depth + z) * 4 * CH, 4 * CH), :] = jnp.concatenate(parts, axis=0).astype(BF16)

    def spread(hidden):
        hid = hidden.shape[0] // depth
        for d1 in range(3):
            for d2 in range(3):
                moved = tap(hidden, d1 - 1, d2 - 1).astype(BF16)
                for z in range(depth):
                    px2[pl.ds(((d1 * depth + z) * 3 + d2) * hid, hid), :] = moved[z * hid : (z + 1) * hid]

    one = jnp.dot(pw1[...], px1[...], preferred_element_type=F32)
    spread(jnp.where(grid_mask, jnp.maximum(one, 0.0), 0.0))
    two = jnp.dot(pw2[...], px2[...], preferred_element_type=F32)
    spread(jnp.where(grid_mask, jnp.maximum(two, 0.0), 0.0))
    three = jnp.dot(pw3[...], px2[...], preferred_element_type=F32)
    updated = field.reshape(depth * CH, lanes) + three
    updated = updated[:, edge : edge + pixels].astype(BF16).astype(F32)
    nv[...] = updated.reshape(depth, CH, pixels)
    leading = jnp.concatenate([updated[z * CH : z * CH + 1] for z in range(depth)], axis=0).astype(BF16)
    windows = jnp.dot(leading, table[...], preferred_element_type=F32).astype(BF16)
    wsend[:, reach_a * group : (reach_a + wide) * group] = windows

    def a_copy(k, row, target):
        lanes_of = pl.ds(pl.multiple_of(target * group, 128), cover)
        return pltpu.make_async_remote_copy(
            src_ref=wsend.at[:, lanes_of],
            dst_ref=arrived.at[row],
            send_sem=a_send.at[k - 1],
            recv_sem=a_recv.at[k - 1],
            device_id=(target, s),
            device_id_type=MESH,
        )

    for k in range(1, wide):
        a_copy(k, w, lax.rem(w + k, wide)).start()
    arrived[w] = wsend[:, pl.ds(pl.multiple_of(w * group, 128), cover)]

    mine = [nv[s * slices + z] for z in range(slices)]
    for c in range(mem):
        vol_out[c] = jnp.concatenate([m[c : c + 1] for m in mine], axis=0).astype(BF16)
    proj[...] = jnp.zeros_like(proj)
    cut[...] = jnp.zeros_like(cut)
    for i, j in d_moves:

        @pl.when(inside(w - i, s - j))
        def _():
            d_copy(i, j, (w, s)).wait_recv()

    for k in range(1, wide):
        a_copy(k, lax.rem(w + wide - k, wide), w).wait_recv()

    for a in range(wide_angles):
        at = (a - HALO + reach_a * angles) * window

        def place(g, carry):
            if groups > 1:
                select(a, g)
            halves = [arrived[g * batch + t].astype(F32)[:, at : at + window] for t in range(batch)]
            return carry + jnp.dot(
                jnp.concatenate(halves, axis=1).astype(BF16), chosen[a], preferred_element_type=F32
            )

        placed = jnp.zeros((depth, bins), F32)
        placed = place(0, placed) if groups == 1 else lax.fori_loop(0, groups, place, placed)
        scaled = (placed * (1.0 / math.sqrt(NY))).astype(BF16).astype(F32)
        for z in range(depth):
            proj[HALO + z, a : a + 1, :] = scaled[z : z + 1]

    lane = lax.broadcasted_iota(jnp.int32, (1, bins), 1)
    row8 = lax.broadcasted_iota(jnp.int32, (CH, bins), 0)
    low, high = lane > 0, lane < bins - 1
    blank = jnp.zeros((CH, bins), F32)

    def three(value):
        return (
            jnp.where(low, shifted(value, -1), 0.0),
            value,
            jnp.where(high, shifted(value, 1), 0.0),
        )

    for a in range(wide_angles):
        for z in range(deep):
            line = proj[s * slices + z, a : a + 1, :]
            value = jnp.where(row8 == 5, line, dual_in[a, z].astype(F32))
            left, mid, right = three(value)
            x1[pl.ds((a * deep + z) * 4 * CH, 4 * CH), :] = jnp.concatenate(
                [left, mid, right, blank], axis=0
            ).astype(BF16)

    def layer(weight, source, dest, out_angles, in_slices, per_slice, margin):
        out_slices = in_slices - 2
        hid = weight.shape[0] // out_slices
        rows = in_slices * per_slice
        row_z = s * slices - margin + lax.broadcasted_iota(jnp.int32, (hid * out_slices, 1), 0) // hid
        z_ok = (row_z >= 0) & (row_z < depth)
        for a in range(out_angles):
            angle = w * angles - margin + a
            ok = z_ok & (angle >= 0) & (angle < angle_total)
            value = jnp.dot(weight[...], source[pl.ds(a * rows, 3 * rows), :], preferred_element_type=F32)
            value = jnp.where(ok, jnp.maximum(value, 0.0), 0.0)
            for d2, moved in enumerate(three(value)):
                moved = moved.astype(BF16)
                for z in range(out_slices):
                    dest[pl.ds(((a * out_slices + z) * 3 + d2) * hid, hid), :] = moved[z * hid : (z + 1) * hid]

    hidden = dw2.shape[0] // (deep - 4)
    layer(dw1, x1, x2, wide_angles - 2, deep, 4 * CH, 2)
    layer(dw2, x2, x3, wide_angles - 4, deep - 2, 3 * hidden, 1)
    rows = (deep - 4) * 3 * hidden
    for a in range(angles):
        value = jnp.dot(dw3[...], x3[pl.ds(a * rows, 3 * rows), :], preferred_element_type=F32)
        own = dual_in[HALO + a, HALO : HALO + slices].astype(F32).reshape(slices * CH, bins)
        value = (own + value).astype(BF16).astype(F32)
        nd[a] = value
        for z in range(slices):
            cut[a, z : z + 1, :] = value[z * CH : z * CH + 1]

    def take(g, carry):
        found = []
        for a in range(angles):
            if groups > 1:
                select(HALO + a, g)
            found.append(
                lax.dot_general(
                    cut[a].astype(BF16), chosen[HALO + a], (((1,), (1,)), ((), ())), preferred_element_type=F32
                )
            )
        for t in range(batch):
            pieces[g * batch + t] = jnp.concatenate(
                [f[:, t * window : (t + 1) * window] for f in found], axis=1
            )
        return carry

    if groups == 1:
        take(0, 0)
    else:
        lax.fori_loop(0, groups, take, 0)

    def b_copy(k, row, target):
        return pltpu.make_async_remote_copy(
            src_ref=pieces.at[target],
            dst_ref=returned.at[row],
            send_sem=b_send.at[k - 1],
            recv_sem=b_recv.at[k - 1],
            device_id=(target, s),
            device_id_type=MESH,
        )

    for k in range(1, wide):
        b_copy(k, w, lax.rem(w + k, wide)).start()
    returned[w] = pieces[w]
    for z in range(slices):
        for c in range(mem):
            lines = [nd[a, z * CH + c : z * CH + c + 1, :] for a in range(angles)]
            dual_out[c, z] = jnp.concatenate(lines, axis=0).astype(BF16)
    for k in range(1, wide):
        b_copy(k, lax.rem(w + wide - k, wide), w).wait_recv()
    lines = jnp.concatenate([returned[t] for t in range(wide)], axis=1).astype(BF16)
    summed = lax.dot_general(lines, table[...], (((1,), (1,)), ((), ())), preferred_element_type=F32)
    back_out[...] = summed[:slices] * (1.0 / math.sqrt(angle_total))
    for k in range(1, wide):
        b_copy(k, w, lax.rem(w + k, wide)).wait_send()
    for i, j in p_moves:

        @pl.when(inside(w + i, s + j))
        def _():
            p_copy(i, j, s, (w, s)).wait_send()

    for i, j in d_moves:

        @pl.when(inside(w + i, s + j))
        def _():
            d_copy(i, j, (w, s)).wait_send()

    for k in range(1, wide):
        a_copy(k, w, lax.rem(w + k, wide)).wait_send()


def split_band(weights, stage, out, out_slices, o_pad):
    c_in, c_out = weights.shape[3:]
    block = 3 * c_in
    chunk = (out_slices + 2) * block
    width = -(-chunk // 128) * 128
    held = -(-3 * block // 128) * 128
    for d1 in range(3):
        stage[...] = jnp.zeros_like(stage)
        for d0 in range(3):
            for d2 in range(3):
                at = (d0 * 3 + d2) * c_in
                stage[at : at + c_in, :c_out] = weights[d0, d1, d2].astype(F32)
        flat = stage[:held, :].T[:o_pad]
        if width > held:
            flat = jnp.concatenate([flat, jnp.zeros((o_pad, width - held), F32)], axis=1)
        for z in range(out_slices):
            row = pltpu.roll(flat, z * block, axis=1) if z else flat
            out[(d1 * out_slices + z) * o_pad : (d1 * out_slices + z + 1) * o_pad, :] = row[:, :chunk].astype(BF16)


def split_taps(weights, out, out_slices):
    c_out, _, c_in = weights.shape[2:]
    width = (out_slices + 2) * c_in
    held = -(-width // 128) * 128
    for d1 in range(3):
        for d2 in range(3):
            lines = [weights[d0, d1, :, d2, :].astype(F32) for d0 in range(3)]
            flat = jnp.concatenate(lines + [jnp.zeros((c_out, held - 3 * c_in), F32)], axis=1)
            flat = jnp.concatenate([flat, jnp.zeros((CH - c_out, held), F32)], axis=0)
            rows = [pltpu.roll(flat, z * c_in, axis=1) if z else flat for z in range(out_slices)]
            at = (d1 * 3 + d2) * out_slices * CH
            out[at : at + out_slices * CH, :] = jnp.concatenate(rows, axis=0)[:, :width].astype(BF16)


def block_kernel(
    wide, slab, *refs
):
    given = refs[:12]
    vol_out, dual_out, back_out = refs[12:15]
    held, in_sem = refs[15:27], refs[27]
    volume, back_proj, dual_state, sinogram, offsets, p1, p2, p3, d1_w, d2_w, d3_w, trig = held
    (
        psrc, dsrc, frame, stack, arrived, windows, table, stage, pw1, pw2, pw3, dw1, dw2, dw3,
        px1, px2, nv, deck, proj, x1, x2, x3, mine_out, cut_out, mine_in, cut_in, begins,
        p_send, p_recv, d_send, d_recv, e_send, e_recv, a_send, a_recv, b_send, b_recv,
    ) = refs[28:]
    w = lax.axis_index("wide")
    s = lax.axis_index("slab")
    mem, slices, pixels = volume.shape
    angles, bins = dual_state.shape[2:]
    angle_total = angles * wide
    depth = slices * slab
    edge = 4 * NY
    lanes = pixels + 2 * edge
    window = NY + 2 * TX
    hidden_channels = p1.shape[4]
    deep = slices + 2 * HALO
    reach_z, span_z = spans(slices)
    block = bins // wide
    broad = block + 128
    stride = block + 2 * MARGIN
    used = angle_total * stride
    total_lanes = deck.shape[1]

    def inside(i, j):
        return (i >= 0) & (i < wide) & (j >= 0) & (j < slab)

    frame[...] = jnp.zeros_like(frame)
    stack[...] = jnp.zeros_like(stack)

    greet = [(i, j) for i in (-1, 0, 1) for j in range(-(slab - 1), slab) if (i, j) != (0, 0)]
    barrier = pltpu.get_barrier_semaphore()
    total = jnp.int32(wide - 1)
    for i, j in greet:
        there = inside(w + i, s + j)

        @pl.when(there)
        def _():
            pl.semaphore_signal(barrier, inc=1, device_id=(w + i, s + j), device_id_type=MESH)

        total = total + jnp.where(there, 1, 0)
    for k in range(1, wide):
        pl.semaphore_signal(barrier, inc=1, device_id=(lax.rem(w + k, wide), s), device_id_type=MESH)

    loads = [pltpu.make_async_copy(src, dst, in_sem.at[n]) for n, (src, dst) in enumerate(zip(given, held))]
    for load in loads:
        load.start()
    deck[...] = jnp.zeros_like(deck)
    proj[...] = jnp.zeros_like(proj)
    for load in loads[:4]:
        load.wait()
    for z in range(slices):
        lines = [volume[c].astype(F32)[z : z + 1] for c in range(mem)]
        lines += [back_proj[z : z + 1, :], jnp.zeros((CH - mem - 1, pixels), F32)]
        psrc[z] = jnp.concatenate(lines, axis=0).astype(BF16)
        for a in range(angles):
            lines = [dual_state[c, z].astype(F32)[a : a + 1] for c in range(mem)]
            lines += [jnp.zeros((1, bins), F32), sinogram[z].astype(F32)[a : a + 1]]
            lines += [jnp.zeros((CH - mem - 2, bins), F32)]
            line = jnp.concatenate([jnp.concatenate(lines, axis=0), jnp.zeros((CH, 128), F32)], axis=1)
            dsrc[a, z] = pltpu.roll(line, 64, axis=1).astype(BF16)
    frame[pl.ds(s * slices, slices), :, edge : edge + pixels] = psrc[...]
    stack[pl.ds(w * angles, angles), HALO : HALO + slices] = dsrc[
        :, :, :, pl.ds(pl.multiple_of(w * block, 128), broad)
    ]
    pl.semaphore_wait(barrier, total)

    def p_copy(i, j, row, target):
        if i == 0:
            src, dst = pl.ds(0, pixels), pl.ds(edge, pixels)
        elif i > 0:
            src, dst = pl.ds(pixels - edge, edge), pl.ds(0, edge)
        else:
            src, dst = pl.ds(0, edge), pl.ds(edge + pixels, edge)
        return pltpu.make_async_remote_copy(
            src_ref=psrc.at[:, :, src],
            dst_ref=frame.at[pl.ds(row * slices, slices), :, dst],
            send_sem=p_send.at[i + 1, j + slab - 1],
            recv_sem=p_recv.at[i + 1, j + slab - 1],
            device_id=target,
            device_id_type=MESH,
        )

    def d_copy(k, row, target):
        return pltpu.make_async_remote_copy(
            src_ref=dsrc.at[:, :, :, pl.ds(pl.multiple_of(target * block, 128), broad)],
            dst_ref=stack.at[pl.ds(row * angles, angles), pl.ds(HALO, slices)],
            send_sem=d_send.at[k - 1],
            recv_sem=d_recv.at[k - 1],
            device_id=(target, s),
            device_id_type=MESH,
        )

    def e_copy(j, target):
        z0, zn, zd = span_z[j]
        return pltpu.make_async_remote_copy(
            src_ref=stack.at[:, pl.ds(HALO + z0, zn)],
            dst_ref=stack.at[:, pl.ds(zd, zn)],
            send_sem=e_send.at[j + reach_z],
            recv_sem=e_recv.at[j + reach_z],
            device_id=(w, target),
            device_id_type=MESH,
        )

    p_moves = [(i, j) for i in (-1, 0, 1) for j in range(-(slab - 1), slab) if (i, j) != (0, 0)]
    e_moves = [j for j in span_z if j != 0]
    for i, j in p_moves:

        @pl.when(inside(w + i, s + j))
        def _():
            p_copy(i, j, s, (w + i, s + j)).start()

    for k in range(1, wide):
        d_copy(k, w, lax.rem(w + k, wide)).start()
    for load in loads[4:]:
        load.wait()
    build_band(p1, stage, pw1, depth, True, CH, 4, hidden_channels)
    build_band(p2, stage, pw2, depth, True, hidden_channels, 3, hidden_channels)
    build_band(p3, stage, pw3, depth, True, hidden_channels, 3, CH, True)
    begin_columns = offsets[...]
    for a in range(angle_total):
        begins[a] = jnp.broadcast_to(begin_columns[:, a : a + 1], (wide, 128))
    per = 128 // window
    part_of = lax.broadcasted_iota(jnp.int32, (1, 128), 1) // window
    detector = []
    for first in range(0, angle_total, per):
        own = begins[first, pl.ds(w, 1), :]
        for n in range(1, per):
            own = jnp.where(part_of == n, begins[first + n, pl.ds(w, 1), :], own)
        detector.append((lax.broadcasted_iota(jnp.int32, (1, 128), 1) - own) & (window - 1))
    build_table(trig, table, jnp.concatenate(detector, axis=1).astype(F32))
    build_band(d1_w, stage, dw1, deep - 2, False, CH, 4, hidden_channels)
    split_band(d2_w, stage, dw2, deep - 4, hidden_channels)
    split_taps(d3_w, dw3, slices)
    for k in range(1, wide):
        d_copy(k, lax.rem(w + wide - k, wide), w).wait_recv()
    for j in e_moves:

        @pl.when(inside(w, s + j))
        def _():
            e_copy(j, s + j).start()

    for i, j in p_moves:

        @pl.when(inside(w - i, s - j))
        def _():
            p_copy(i, j, s - j, (w, s)).wait_recv()


    plane = lax.broadcasted_iota(jnp.int32, (1, lanes), 1)
    y = plane % NY
    x = w * TX + plane // NY - 4
    grid_mask = (x >= 0) & (x < wide * TX)
    y_mask = {-1: y > 0, 0: None, 1: y < NY - 1}

    def tap(value, d1, d2):
        moved = shifted(value, NY * d1 + d2)
        return moved if d2 == 0 else jnp.where(y_mask[d2], moved, 0.0)

    field = frame[...].astype(F32)
    pblank = jnp.zeros((CH, lanes), F32)
    for z in range(depth):
        for d1 in range(3):
            parts = [tap(field[z], d1 - 1, d2) for d2 in (-1, 0, 1)] + [pblank]
            px1[pl.ds((d1 * depth + z) * 4 * CH, 4 * CH), :] = jnp.concatenate(parts, axis=0).astype(BF16)

    def spread(hidden):
        hid = hidden.shape[0] // depth
        for d1 in range(3):
            for d2 in range(3):
                moved = tap(hidden, d1 - 1, d2 - 1).astype(BF16)
                for z in range(depth):
                    px2[pl.ds(((d1 * depth + z) * 3 + d2) * hid, hid), :] = moved[z * hid : (z + 1) * hid]

    one = jnp.dot(pw1[...], px1[...], preferred_element_type=F32)
    spread(jnp.where(grid_mask, jnp.maximum(one, 0.0), 0.0))
    two = jnp.dot(pw2[...], px2[...], preferred_element_type=F32)
    spread(jnp.where(grid_mask, jnp.maximum(two, 0.0), 0.0))
    three = jnp.dot(pw3[...], px2[...], preferred_element_type=F32)
    updated = field.reshape(depth * CH, lanes) + three
    updated = updated[:, edge : edge + pixels].astype(BF16).astype(F32)
    nv[...] = updated.reshape(depth, CH, pixels)
    leading = jnp.concatenate([updated[z * CH : z * CH + 1] for z in range(depth)], axis=0).astype(BF16)
    windows[...] = jnp.dot(leading, table[...], preferred_element_type=F32).astype(BF16)

    def a_copy(k, row, target):
        return pltpu.make_async_remote_copy(
            src_ref=windows,
            dst_ref=arrived.at[row],
            send_sem=a_send.at[k - 1],
            recv_sem=a_recv.at[k - 1],
            device_id=(target, s),
            device_id_type=MESH,
        )

    for k in range(1, wide):
        a_copy(k, w, lax.rem(w + k, wide)).start()
    arrived[w] = windows[...]

    mine = [nv[s * slices + z] for z in range(slices)]
    for c in range(mem):
        vol_out[c] = jnp.concatenate([m[c : c + 1] for m in mine], axis=0).astype(BF16)
    for j in e_moves:

        @pl.when(inside(w, s - j))
        def _():
            e_copy(j, s).wait_recv()

    skip = 64 - MARGIN
    for a in range(angle_total):
        for z in range(deep):
            value = stack[a, z].astype(F32)[:, skip : skip + stride]
            deck[z * CH : (z + 1) * CH, a * stride : (a + 1) * stride] = value
    for k in range(1, wide):
        a_copy(k, lax.rem(w + wide - k, wide), w).wait_recv()

    at = lax.broadcasted_iota(jnp.int32, (depth, 128), 1)
    bins_at = [at + (w * block - 64 + n * 128) for n in range(broad // 128)]
    for first in range(0, angle_total, per):
        placed = [[jnp.zeros((depth, 128), F32) for _ in bins_at] for _ in range(per)]
        for t in range(wide):
            source = arrived[t, :, first * window : first * window + 128].astype(F32)
            for n in range(per):
                line = source
                for m in range(per):
                    if m != n:
                        line = jnp.where(at // window == m, pltpu.roll(source, (m - n) * window % 128, axis=1), line)
                begin = begins[first + n, t : t + 1, :]
                for m, bin_of in enumerate(bins_at):
                    inner = bin_of - begin
                    placed[n][m] = placed[n][m] + jnp.where((inner >= 0) & (inner < window), line, 0.0)
        for n in range(per):
            line = jnp.concatenate(placed[n], axis=1) * (1.0 / math.sqrt(NY))
            line = line.astype(BF16).astype(F32)[:, skip : skip + stride]
            proj[8 : 8 + depth, (first + n) * stride : (first + n + 1) * stride] = line

    lane = lax.broadcasted_iota(jnp.int32, (1, total_lanes), 1)
    begin = jnp.zeros_like(lane)
    for a in range(1, angle_total):
        begin = jnp.where(lane >= a * stride, a * stride, begin)
    bin_at = w * block - MARGIN + lane - begin
    lane_ok = (lane < used) & (bin_at >= 0) & (bin_at < bins)
    row8 = lax.broadcasted_iota(jnp.int32, (CH, total_lanes), 0)
    blank = jnp.zeros((CH, total_lanes), F32)
    for z in range(deep):
        line = proj[pl.ds(8 - HALO + s * slices + z, 1), :]
        value = jnp.where(row8 == mem, line, deck[z * CH : (z + 1) * CH, :])
        for d1 in range(3):
            parts = [shifted(value, (d1 - 1) * stride + d2 - 1) for d2 in range(3)] + [blank]
            x1[(d1 * deep + z) * 4 * CH : (d1 * deep + z + 1) * 4 * CH, :] = jnp.concatenate(parts, axis=0).astype(BF16)

    def kept(value, out_slices, margin):
        hid = value.shape[0] // out_slices
        row_z = s * slices - margin + lax.broadcasted_iota(jnp.int32, (value.shape[0], 1), 0) // hid
        return jnp.where((row_z >= 0) & (row_z < depth) & lane_ok, jnp.maximum(value, 0.0), 0.0)

    hid = hidden_channels
    value = kept(jnp.dot(dw1[...], x1[...], preferred_element_type=F32), deep - 2, 2)
    for d2 in range(3):
        moved = shifted(value, d2 - 1).astype(BF16)
        for z in range(deep - 2):
            x2[(z * 3 + d2) * hid : (z * 3 + d2 + 1) * hid, :] = moved[z * hid : (z + 1) * hid]
    rows = (deep - 4) * hid
    value = jnp.zeros((rows, total_lanes), F32)
    for d1 in range(3):
        part = jnp.dot(dw2[d1 * rows : (d1 + 1) * rows, :], x2[...], preferred_element_type=F32)
        value = value + shifted(part, (d1 - 1) * stride)
    x3[...] = kept(value, deep - 4, 1).astype(BF16)
    part = jnp.dot(dw3[...], x3[...], preferred_element_type=F32)
    rows = slices * CH
    value = deck[HALO * CH : HALO * CH + rows, :]
    for d1 in range(3):
        for d2 in range(3):
            n = d1 * 3 + d2
            value = value + shifted(part[n * rows : (n + 1) * rows], (d1 - 1) * stride + d2 - 1)
    value = value.astype(BF16).astype(F32)
    heads = []
    for a in range(angle_total):
        own = value[:, a * stride + MARGIN : a * stride + MARGIN + block]
        mine_out[a] = own.astype(BF16)
        heads += [own[z * CH : z * CH + 1] for z in range(slices)]
    cut_out[...] = jnp.concatenate(heads, axis=0).astype(BF16)

    def b_copy(n, k, row, target):
        lanes_of = pl.ds(pl.multiple_of(row * block, 128), block)
        if n == 0:
            src, dst = cut_out, cut_in.at[:, lanes_of]
        else:
            src, dst = mine_out.at[pl.ds(target * angles, angles)], mine_in.at[:, :, lanes_of]
        return pltpu.make_async_remote_copy(
            src_ref=src,
            dst_ref=dst,
            send_sem=b_send.at[n, k - 1],
            recv_sem=b_recv.at[n, k - 1],
            device_id=(target, s),
            device_id_type=MESH,
        )

    for n in range(2):
        for k in range(1, wide):
            b_copy(n, k, w, lax.rem(w + k, wide)).start()
    lanes_of = pl.ds(pl.multiple_of(w * block, 128), block)
    cut_in[:, lanes_of] = cut_out[...]
    mine_in[:, :, lanes_of] = mine_out[pl.ds(w * angles, angles)]
    for k in range(1, wide):
        b_copy(0, k, lax.rem(w + wide - k, wide), w).wait_recv()
    line8 = lax.broadcasted_iota(jnp.int32, (8, 128), 0)
    lane8 = lax.broadcasted_iota(jnp.int32, (8, 128), 1)
    cut = cut_in[...].astype(F32)
    taken = []
    for first in range(0, angle_total, per):
        joined = jnp.zeros((8, 128), F32)
        for n in range(per):
            a = first + n
            begin = begins[a, pl.ds(w, 1), :]
            group = a * slices // 8 * 8
            found = jnp.zeros((8, 128), F32)
            for m in range(0, bins, 128):
                inner = lane8 + m - begin
                found = jnp.where((inner >= 0) & (inner < window), cut[group : group + 8, m : m + 128], found)
            both = found
            for m in range(1, per):
                both = both + pltpu.roll(found, m * window, axis=1)
            at_row = a * slices - group
            here = (lane8 // window == n) & (line8 >= at_row) & (line8 < at_row + slices)
            joined = jnp.where(here, both, joined)
        taken.append(joined)
    lines = jnp.concatenate(taken, axis=1).astype(BF16)
    summed = lax.dot_general(lines, table[...], (((1,), (1,)), ((), ())), preferred_element_type=F32)
    total_back = summed[:slices]
    for n in range(1, 8 // slices):
        total_back = total_back + summed[n * slices : (n + 1) * slices]
    back_out[...] = total_back * (1.0 / math.sqrt(angle_total))
    for k in range(1, wide):
        b_copy(1, k, lax.rem(w + wide - k, wide), w).wait_recv()
    for z in range(slices):
        for c in range(mem):
            lines = [mine_in[a].astype(F32)[z * CH + c : z * CH + c + 1] for a in range(angles)]
            dual_out[c, z] = jnp.concatenate(lines, axis=0).astype(BF16)
    for k in range(1, wide):
        for n in range(2):
            b_copy(n, k, w, lax.rem(w + k, wide)).wait_send()
    for i, j in p_moves:

        @pl.when(inside(w + i, s + j))
        def _():
            p_copy(i, j, s, (w, s)).wait_send()

    for k in range(1, wide):
        d_copy(k, w, lax.rem(w + k, wide)).wait_send()
    for j in e_moves:

        @pl.when(inside(w, s + j))
        def _():
            e_copy(j, s + j).wait_send()

    for k in range(1, wide):
        a_copy(k, w, lax.rem(w + k, wide)).wait_send()


def hand_on(outs):
    def kernel(*refs):
        for src, dst in zip(refs[:3], refs[3:]):
            dst[...] = src[...]

    space = pl.BlockSpec(memory_space=pltpu.VMEM)
    return pl.pallas_call(
        kernel,
        out_shape=tuple(jax.ShapeDtypeStruct(o.shape, o.dtype) for o in outs),
        in_specs=[space] * 3,
        out_specs=(space,) * 3,
        name="hand_on",
    )(*outs)


def block_body(wide, slab, volume, back_proj, dual_state, sinogram, offsets, p1, p2, p3, d1, d2, d3):
    mem, slices, pixels = volume.shape
    angles, bins = dual_state.shape[2:]
    depth = slices * slab
    angle_total = angles * wide
    hidden = p1.shape[4]
    reach_z, _ = spans(slices)
    lanes = pixels + 8 * NY
    window = NY + 2 * TX
    block = bins // wide
    stride = block + 2 * MARGIN
    spread_lanes = -(-((angle_total + 1) * stride + 1) // 128) * 128
    deep = slices + 2 * HALO
    dma = pltpu.SemaphoreType.DMA
    vmem = pltpu.VMEM
    space = pl.BlockSpec(memory_space=pltpu.VMEM)
    args = (volume, back_proj, dual_state, sinogram, offsets, p1, p2, p3.transpose(0, 1, 4, 2, 3))
    args += (d1, d2, d3.transpose(0, 1, 4, 2, 3), jnp.asarray(trig_rows(angle_total)))
    outs = pl.pallas_call(
        functools.partial(block_kernel, wide, slab),
        out_shape=(
            jax.ShapeDtypeStruct(volume.shape, BF16),
            jax.ShapeDtypeStruct(dual_state.shape, BF16),
            jax.ShapeDtypeStruct(back_proj.shape, F32),
        ),
        in_specs=[pl.BlockSpec(memory_space=pl.ANY)] * 12,
        out_specs=(space,) * 3,
        scratch_shapes=[vmem(a.shape, a.dtype) for a in args]
        + [dma((12,))]
        + [
            vmem((slices, CH, pixels), BF16),
            vmem((angles, slices, CH, bins + 128), BF16),
            vmem((depth, CH, lanes), BF16),
            vmem((angle_total, deep, CH, block + 128), BF16),
            vmem((wide, depth, angle_total * window), BF16),
            vmem((depth, angle_total * window), BF16),
            vmem((pixels, angle_total * window), BF16),
            vmem((-(-9 * hidden // 128) * 128, 128), F32),
            vmem((depth * hidden, 12 * depth * CH), BF16),
            vmem((depth * hidden, 9 * depth * hidden), BF16),
            vmem((depth * CH, 9 * depth * hidden), BF16),
            vmem(((deep - 2) * hidden, 12 * deep * CH), BF16),
            vmem((3 * (deep - 4) * hidden, 3 * (deep - 2) * hidden), BF16),
            vmem((9 * slices * CH, (deep - 4) * hidden), BF16),
            vmem((12 * depth * CH, lanes), BF16),
            vmem((9 * depth * hidden, lanes), BF16),
            vmem((depth, CH, pixels), F32),
            vmem((deep * CH, spread_lanes), F32),
            vmem((-(-depth // 8) * 8 + 16, spread_lanes), F32),
            vmem((12 * deep * CH, spread_lanes), BF16),
            vmem((3 * (deep - 2) * hidden, spread_lanes), BF16),
            vmem(((deep - 4) * hidden, spread_lanes), BF16),
            vmem((angle_total, slices * CH, block), BF16),
            vmem((angle_total * slices, block), BF16),
            vmem((angles, slices * CH, bins), BF16),
            vmem((angle_total * slices, bins), BF16),
            vmem((angle_total, wide, 128), jnp.int32),
            dma((3, 2 * slab - 1)),
            dma((3, 2 * slab - 1)),
            dma((wide - 1,)),
            dma((wide - 1,)),
            dma((2 * reach_z + 1,)),
            dma((2 * reach_z + 1,)),
            dma((wide - 1,)),
            dma((wide - 1,)),
            dma((2, wide - 1)),
            dma((2, wide - 1)),
        ],
        compiler_params=pltpu.CompilerParams(
            collective_id=0, has_side_effects=True, vmem_limit_bytes=VMEM_LIMIT
        ),
        name="block_kernel",
    )(*args)
    return hand_on(outs)


def body(wide, slab, volume, back_proj, dual_state, sinogram, offsets, p1, p2, p3, d1, d2, d3):
    mem, slices, pixels = volume.shape
    angles, bins = dual_state.shape[2:]
    if bins % (128 * wide) == 0 and 8 % slices == 0 and angles * wide * slices % 16 == 0:
        return block_body(wide, slab, volume, back_proj, dual_state, sinogram, offsets, p1, p2, p3, d1, d2, d3)
    depth = slices * slab
    angle_total = angles * wide
    hidden = p1.shape[4]
    group = angles * (NY + 2 * TX)
    reach_a, _ = spans(angles)
    reach_z, _ = spans(slices)
    lanes = pixels + 8 * NY
    wide_angles = angles + 2 * HALO
    deep = slices + 2 * HALO
    dma = pltpu.SemaphoreType.DMA
    vmem = pltpu.VMEM
    space = pl.BlockSpec(memory_space=pltpu.VMEM)
    args = (volume, back_proj, dual_state, sinogram, offsets, p1, p2, p3.transpose(0, 1, 4, 2, 3))
    args += (d1, d2, d3.transpose(0, 1, 4, 2, 3), jnp.asarray(trig_rows(angle_total)))
    outs = pl.pallas_call(
        functools.partial(whole_kernel, wide, slab),
        out_shape=(
            jax.ShapeDtypeStruct(volume.shape, BF16),
            jax.ShapeDtypeStruct(dual_state.shape, BF16),
            jax.ShapeDtypeStruct(back_proj.shape, F32),
        ),
        in_specs=[pl.BlockSpec(memory_space=pl.ANY)] * 12,
        out_specs=(space,) * 3,
        scratch_shapes=[vmem(a.shape, a.dtype) for a in args]
        + [dma((12,))]
        + [
            vmem((slices, CH, pixels), BF16),
            vmem((angles, slices, CH, bins), BF16),
            vmem((depth, CH, lanes), BF16),
            vmem((wide_angles, deep, CH, bins), BF16),
            vmem((wide, depth, (2 * reach_a + 1) * group), BF16),
            vmem((depth, (wide + 2 * reach_a) * group), BF16),
            vmem((pixels, angle_total * (NY + 2 * TX)), BF16),
            vmem((-(-9 * hidden // 128) * 128, 128), F32),
            vmem((depth * hidden, 12 * depth * CH), BF16),
            vmem((depth * hidden, 9 * depth * hidden), BF16),
            vmem((depth * CH, 9 * depth * hidden), BF16),
            vmem(((deep - 2) * hidden, 12 * deep * CH), BF16),
            vmem(((deep - 4) * hidden, 9 * (deep - 2) * hidden), BF16),
            vmem(((deep - 6) * CH, 9 * (deep - 4) * hidden), BF16),
            vmem((12 * depth * CH, lanes), BF16),
            vmem((9 * depth * hidden, lanes), BF16),
            vmem((depth, CH, pixels), F32),
            vmem((wide_angles, math.gcd(wide, 8) * (NY + 2 * TX), bins), BF16),
            vmem((depth + 2 * HALO, wide_angles, bins), F32),
            vmem((wide_angles * deep * 4 * CH, bins), BF16),
            vmem(((wide_angles - 2) * (deep - 2) * 3 * hidden, bins), BF16),
            vmem(((wide_angles - 4) * (deep - 4) * 3 * hidden, bins), BF16),
            vmem((angles, slices * CH, bins), F32),
            vmem((angles, 8, bins), F32),
            vmem((wide, 8, group), F32),
            vmem((wide, 8, group), F32),
            dma((3, 2 * slab - 1)),
            dma((3, 2 * slab - 1)),
            dma((2 * reach_a + 1, 2 * reach_z + 1)),
            dma((2 * reach_a + 1, 2 * reach_z + 1)),
            dma((wide - 1,)),
            dma((wide - 1,)),
            dma((wide - 1,)),
            dma((wide - 1,)),
        ],
        compiler_params=pltpu.CompilerParams(
            collective_id=0, has_side_effects=True, vmem_limit_bytes=VMEM_LIMIT
        ),
        name="whole_kernel",
    )(*args)
    return hand_on(outs)


def solution(mesh):
    wide, slab = mesh.shape["wide"], mesh.shape["slab"]
    in_specs = (
        P(None, "slab", "wide"),
        P("slab", "wide"),
        P(None, "slab", "wide", None),
        P("slab", "wide", None),
    ) + (P(),) * 7
    out_specs = (P(None, "slab", "wide"), P(None, "slab", "wide", None), P("slab", "wide"))
    return jax.shard_map(
        functools.partial(body, wide, slab), mesh=mesh, in_specs=in_specs, out_specs=out_specs, check_vma=False
    )
```

```python
import functools
import math

import jax
import jax.numpy as jnp
import numpy as np
from jax import lax
from jax.experimental import pallas as pl
from jax.experimental.pallas import tpu as pltpu
from jax.sharding import PartitionSpec as P

NY = 32
TX = 16
HALO = 3
CH = 8
MARGIN = HALO
MESH = pl.DeviceIdType.MESH
F32 = jnp.float32
BF16 = jnp.bfloat16
VMEM_LIMIT = 60 * 1024 * 1024


def trig_rows(angle_total):
    window = NY + 2 * TX
    angle = np.arange(angle_total, dtype=np.float32) * np.float32(math.pi / angle_total)
    rows = np.zeros((8, angle_total * window), np.float32)
    rows[0] = np.repeat(np.cos(angle), window)
    rows[1] = np.repeat(np.sin(angle), window)
    rows[2] = np.tile(np.arange(window, dtype=np.float32), angle_total)
    return rows


def build_table(trig, table, detector=None):
    cosine, sine = trig[0:1, :], trig[1:2, :]
    detector = trig[2:3, :] if detector is None else detector
    centre_y = lax.broadcasted_iota(jnp.int32, (NY, trig.shape[1]), 0).astype(F32) - (NY - 1) / 2.0

    def row(i, carry):
        centre_x = lax.convert_element_type(i, F32) - (TX - 1) / 2.0
        positions = centre_x * cosine + centre_y * sine + (NY + 2 * TX) / 2.0
        value = jnp.maximum(0.0, 1.0 - jnp.abs(positions - detector))
        table[pl.ds(pl.multiple_of(i * NY, NY), NY), :] = value.astype(BF16)
        return carry

    lax.fori_loop(0, TX, row, 0)


def build_band(weights, stage, out, out_slices, same, c_pad, bin_pad, o_pad, turn=False):
    if turn:
        c_out, _, c_in = weights.shape[2:]
    else:
        c_in, c_out = weights.shape[3:]
    block = bin_pad * c_pad
    in_slices = out_slices if same else out_slices + 2
    chunk = in_slices * block
    width = chunk if chunk % 128 == 0 else -(-3 * chunk // 128) * 128
    held = -(-3 * block // 128) * 128
    pieces = []
    for d1 in range(3):
        if turn:
            lines = []
            for d0 in range(3):
                lines += [weights[d0, d1, :, d2, :].astype(F32) for d2 in range(3)]
            flat = jnp.concatenate(lines + [jnp.zeros((c_out, held - 9 * c_in), F32)], axis=1)
            flat = jnp.concatenate([flat, jnp.zeros((o_pad - c_out, held), F32)], axis=0)
        else:
            stage[...] = jnp.zeros_like(stage)
            for d0 in range(3):
                for d2 in range(3):
                    at = (d0 * bin_pad + d2) * c_pad
                    stage[at : at + c_in, :c_out] = weights[d0, d1, d2].astype(F32)
            flat = stage[:held, :].T[:o_pad]
        if width > held:
            flat = jnp.concatenate([flat, jnp.zeros((o_pad, width - held), F32)], axis=1)
        pieces.append(flat[:, :width])
    lane = lax.broadcasted_iota(jnp.int32, (1, width), 1)

    def turned(piece, by):
        by = by % width
        return pltpu.roll(piece, by, axis=1) if by else piece

    waiting = []
    for z in range(out_slices):
        if chunk % 128 == 0:
            parts = []
            for piece in pieces:
                part = turned(piece, (z - 1 if same else z) * block)
                if same and z == 0:
                    part = jnp.where(lane < 2 * block, part, 0.0)
                if same and z == out_slices - 1:
                    part = jnp.where(lane >= (z - 1) * block, part, 0.0)
                parts.append(part)
            row = jnp.concatenate(parts, axis=1)
        else:
            assert not same
            row = sum(turned(piece, d1 * chunk + z * block) for d1, piece in enumerate(pieces))
        waiting.append(row)
        rows = len(waiting) * o_pad
        if rows % 16 == 0:
            both = waiting[0] if len(waiting) == 1 else jnp.concatenate(waiting, axis=0)
            out[(z + 1) * o_pad - rows : (z + 1) * o_pad, :] = both[:, : 3 * chunk].astype(BF16)
            waiting = []
    assert not waiting


def shifted(value, by):
    lanes = value.shape[-1]
    return value if by == 0 else pltpu.roll(value, (-by) % lanes, axis=value.ndim - 1)


def spans(block):
    reach = -(-HALO // block)
    result = {}
    for d in range(-reach, reach + 1):
        count = block if d == 0 else min(block, HALO - (abs(d) - 1) * block)
        first = block - count if d > 0 else 0
        result[d] = (first, count, first - d * block + HALO)
    return reach, result


def whole_kernel(
    wide, slab, *refs
):
    given = refs[:12]
    vol_out, dual_out, back_out = refs[12:15]
    held, in_sem = refs[15:27], refs[27]
    volume, back_proj, dual_state, sinogram, offsets, p1, p2, p3, d1_w, d2_w, d3_w, trig = held
    (
    psrc, dsrc, frame, dual_in, arrived, wsend, table, stage, pw1, pw2, pw3, dw1, dw2, dw3,
    px1, px2, nv, chosen, proj, x1, x2, x3, nd, cut, pieces, returned,
    p_send, p_recv, d_send, d_recv, a_send, a_recv, b_send, b_recv,
    ) = refs[28:]
    w = lax.axis_index("wide")
    s = lax.axis_index("slab")
    mem, slices, pixels = volume.shape
    angles, bins = dual_state.shape[2:]
    angle_total = angles * wide
    depth = slices * slab
    edge = 4 * NY
    lanes = pixels + 2 * edge
    window = NY + 2 * TX
    hidden_channels = p1.shape[4]
    wide_angles = angles + 2 * HALO
    deep = slices + 2 * HALO
    reach_a, span_a = spans(angles)
    reach_z, span_z = spans(slices)
    group = angles * window
    cover = (2 * reach_a + 1) * group

    def inside(i, j):
        return (i >= 0) & (i < wide) & (j >= 0) & (j < slab)

    frame[...] = jnp.zeros_like(frame)
    dual_in[...] = jnp.zeros_like(dual_in)

    reach_w = max(1, reach_a)
    greet = [
        (i, j) for i in range(-reach_w, reach_w + 1) for j in range(-(slab - 1), slab) if (i, j) != (0, 0)
    ]
    barrier = pltpu.get_barrier_semaphore()
    total = jnp.int32(wide - 1)
    for i, j in greet:
        there = inside(w + i, s + j)

        @pl.when(there)
        def _():
            pl.semaphore_signal(barrier, inc=1, device_id=(w + i, s + j), device_id_type=MESH)

        total = total + jnp.where(there, 1, 0)
    for k in range(1, wide):
        pl.semaphore_signal(barrier, inc=1, device_id=(lax.rem(w + k, wide), s), device_id_type=MESH)

    loads = [pltpu.make_async_copy(src, dst, in_sem.at[n]) for n, (src, dst) in enumerate(zip(given, held))]
    for load in loads:
        load.start()
    wsend[...] = jnp.zeros_like(wsend)
    for load in loads[:4]:
        load.wait()
    for z in range(slices):
        lines = [volume[c].astype(F32)[z : z + 1] for c in range(mem)]
        lines += [back_proj[z : z + 1, :], jnp.zeros((CH - mem - 1, pixels), F32)]
        psrc[z] = jnp.concatenate(lines, axis=0).astype(BF16)
        for a in range(angles):
            lines = [dual_state[c, z].astype(F32)[a : a + 1] for c in range(mem)]
            lines += [jnp.zeros((1, bins), F32), sinogram[z].astype(F32)[a : a + 1]]
            lines += [jnp.zeros((CH - mem - 2, bins), F32)]
            dsrc[a, z] = jnp.concatenate(lines, axis=0).astype(BF16)
    frame[pl.ds(s * slices, slices), :, edge : edge + pixels] = psrc[...]
    dual_in[HALO : HALO + angles, HALO : HALO + slices] = dsrc[...]
    pl.semaphore_wait(barrier, total)

    def p_copy(i, j, row, target):
        if i == 0:
            src, dst = pl.ds(0, pixels), pl.ds(edge, pixels)
        elif i > 0:
            src, dst = pl.ds(pixels - edge, edge), pl.ds(0, edge)
        else:
            src, dst = pl.ds(0, edge), pl.ds(edge + pixels, edge)
        return pltpu.make_async_remote_copy(
            src_ref=psrc.at[:, :, src],
            dst_ref=frame.at[pl.ds(row * slices, slices), :, dst],
            send_sem=p_send.at[i + 1, j + slab - 1],
            recv_sem=p_recv.at[i + 1, j + slab - 1],
            device_id=target,
            device_id_type=MESH,
        )

    def d_copy(i, j, target):
        a0, an, ad = span_a[i]
        z0, zn, zd = span_z[j]
        return pltpu.make_async_remote_copy(
            src_ref=dsrc.at[pl.ds(a0, an), pl.ds(z0, zn)],
            dst_ref=dual_in.at[pl.ds(ad, an), pl.ds(zd, zn)],
            send_sem=d_send.at[i + reach_a, j + reach_z],
            recv_sem=d_recv.at[i + reach_a, j + reach_z],
            device_id=target,
            device_id_type=MESH,
        )

    p_moves = [(i, j) for i in (-1, 0, 1) for j in range(-(slab - 1), slab) if (i, j) != (0, 0)]
    d_moves = [(i, j) for i in span_a for j in span_z if (i, j) != (0, 0)]
    for i, j in p_moves:

        @pl.when(inside(w + i, s + j))
        def _():
            p_copy(i, j, s, (w + i, s + j)).start()

    for i, j in d_moves:

        @pl.when(inside(w + i, s + j))
        def _():
            d_copy(i, j, (w + i, s + j)).start()


    for load in loads[4:]:
        load.wait()
    batch = math.gcd(wide, 8)
    groups = wide // batch
    relative = lax.broadcasted_iota(jnp.int32, (window, bins), 1) - lax.broadcasted_iota(
        jnp.int32, (window, bins), 0
    )

    def select(a, g):
        column = jnp.clip(w * angles + a - HALO, 0, angle_total - 1)
        rows = offsets[pl.ds(g * batch, batch), :]
        here = lax.broadcasted_iota(jnp.int32, rows.shape, 1) == column
        begin = jnp.sum(jnp.where(here, rows, 0), axis=1, keepdims=True)
        for t in range(batch):
            hit = relative == begin[t : t + 1]
            chosen[a, t * window : (t + 1) * window, :] = jnp.where(hit, 1.0, 0.0).astype(BF16)

    build_band(p1, stage, pw1, depth, True, CH, 4, hidden_channels)
    build_band(p2, stage, pw2, depth, True, hidden_channels, 3, hidden_channels)
    build_band(p3, stage, pw3, depth, True, hidden_channels, 3, CH, True)
    build_table(trig, table)
    build_band(d1_w, stage, dw1, deep - 2, False, CH, 4, hidden_channels)
    build_band(d2_w, stage, dw2, deep - 4, False, hidden_channels, 3, hidden_channels)
    build_band(d3_w, stage, dw3, deep - 6, False, hidden_channels, 3, CH, True)
    if groups == 1:
        for a in range(wide_angles):
            select(a, 0)

    for i, j in p_moves:

        @pl.when(inside(w - i, s - j))
        def _():
            p_copy(i, j, s - j, (w, s)).wait_recv()


    plane = lax.broadcasted_iota(jnp.int32, (1, lanes), 1)
    y = plane % NY
    x = w * TX + plane // NY - 4
    grid_mask = (x >= 0) & (x < wide * TX)
    y_mask = {-1: y > 0, 0: None, 1: y < NY - 1}

    def tap(value, d1, d2):
        moved = shifted(value, NY * d1 + d2)
        return moved if d2 == 0 else jnp.where(y_mask[d2], moved, 0.0)

    field = frame[...].astype(F32)
    pblank = jnp.zeros((CH, lanes), F32)
    for z in range(depth):
        for d1 in range(3):
            parts = [tap(field[z], d1 - 1, d2) for d2 in (-1, 0, 1)] + [pblank]
            px1[pl.ds((d1 * depth + z) * 4 * CH, 4 * CH), :] = jnp.concatenate(parts, axis=0).astype(BF16)

    def spread(hidden):
        hid = hidden.shape[0] // depth
        for d1 in range(3):
            for d2 in range(3):
                moved = tap(hidden, d1 - 1, d2 - 1).astype(BF16)
                for z in range(depth):
                    px2[pl.ds(((d1 * depth + z) * 3 + d2) * hid, hid), :] = moved[z * hid : (z + 1) * hid]

    one = jnp.dot(pw1[...], px1[...], preferred_element_type=F32)
    spread(jnp.where(grid_mask, jnp.maximum(one, 0.0), 0.0))
    two = jnp.dot(pw2[...], px2[...], preferred_element_type=F32)
    spread(jnp.where(grid_mask, jnp.maximum(two, 0.0), 0.0))
    three = jnp.dot(pw3[...], px2[...], preferred_element_type=F32)
    updated = field.reshape(depth * CH, lanes) + three
    updated = updated[:, edge : edge + pixels].astype(BF16).astype(F32)
    nv[...] = updated.reshape(depth, CH, pixels)
    leading = jnp.concatenate([updated[z * CH : z * CH + 1] for z in range(depth)], axis=0).astype(BF16)
    windows = jnp.dot(leading, table[...], preferred_element_type=F32).astype(BF16)
    wsend[:, reach_a * group : (reach_a + wide) * group] = windows

    def a_copy(k, row, target):
        lanes_of = pl.ds(pl.multiple_of(target * group, 128), cover)
        return pltpu.make_async_remote_copy(
            src_ref=wsend.at[:, lanes_of],
            dst_ref=arrived.at[row],
            send_sem=a_send.at[k - 1],
            recv_sem=a_recv.at[k - 1],
            device_id=(target, s),
            device_id_type=MESH,
        )

    for k in range(1, wide):
        a_copy(k, w, lax.rem(w + k, wide)).start()
    arrived[w] = wsend[:, pl.ds(pl.multiple_of(w * group, 128), cover)]

    mine = [nv[s * slices + z] for z in range(slices)]
    for c in range(mem):
        vol_out[c] = jnp.concatenate([m[c : c + 1] for m in mine], axis=0).astype(BF16)
    proj[...] = jnp.zeros_like(proj)
    cut[...] = jnp.zeros_like(cut)
    for i, j in d_moves:

        @pl.when(inside(w - i, s - j))
        def _():
            d_copy(i, j, (w, s)).wait_recv()

    for k in range(1, wide):
        a_copy(k, lax.rem(w + wide - k, wide), w).wait_recv()

    for a in range(wide_angles):
        at = (a - HALO + reach_a * angles) * window

        def place(g, carry):
            if groups > 1:
                select(a, g)
            halves = [arrived[g * batch + t].astype(F32)[:, at : at + window] for t in range(batch)]
            return carry + jnp.dot(
                jnp.concatenate(halves, axis=1).astype(BF16), chosen[a], preferred_element_type=F32
            )

        placed = jnp.zeros((depth, bins), F32)
        placed = place(0, placed) if groups == 1 else lax.fori_loop(0, groups, place, placed)
        scaled = (placed * (1.0 / math.sqrt(NY))).astype(BF16).astype(F32)
        for z in range(depth):
            proj[HALO + z, a : a + 1, :] = scaled[z : z + 1]

    lane = lax.broadcasted_iota(jnp.int32, (1, bins), 1)
    row8 = lax.broadcasted_iota(jnp.int32, (CH, bins), 0)
    low, high = lane > 0, lane < bins - 1
    blank = jnp.zeros((CH, bins), F32)

    def three(value):
        return (
            jnp.where(low, shifted(value, -1), 0.0),
            value,
            jnp.where(high, shifted(value, 1), 0.0),
        )

    for a in range(wide_angles):
        for z in range(deep):
            line = proj[s * slices + z, a : a + 1, :]
            value = jnp.where(row8 == 5, line, dual_in[a, z].astype(F32))
            left, mid, right = three(value)
            x1[pl.ds((a * deep + z) * 4 * CH, 4 * CH), :] = jnp.concatenate(
                [left, mid, right, blank], axis=0
            ).astype(BF16)

    def layer(weight, source, dest, out_angles, in_slices, per_slice, margin):
        out_slices = in_slices - 2
        hid = weight.shape[0] // out_slices
        rows = in_slices * per_slice
        row_z = s * slices - margin + lax.broadcasted_iota(jnp.int32, (hid * out_slices, 1), 0) // hid
        z_ok = (row_z >= 0) & (row_z < depth)
        for a in range(out_angles):
            angle = w * angles - margin + a
            ok = z_ok & (angle >= 0) & (angle < angle_total)
            value = jnp.dot(weight[...], source[pl.ds(a * rows, 3 * rows), :], preferred_element_type=F32)
            value = jnp.where(ok, jnp.maximum(value, 0.0), 0.0)
            for d2, moved in enumerate(three(value)):
                moved = moved.astype(BF16)
                for z in range(out_slices):
                    dest[pl.ds(((a * out_slices + z) * 3 + d2) * hid, hid), :] = moved[z * hid : (z + 1) * hid]

    hidden = dw2.shape[0] // (deep - 4)
    layer(dw1, x1, x2, wide_angles - 2, deep, 4 * CH, 2)
    layer(dw2, x2, x3, wide_angles - 4, deep - 2, 3 * hidden, 1)
    rows = (deep - 4) * 3 * hidden
    for a in range(angles):
        value = jnp.dot(dw3[...], x3[pl.ds(a * rows, 3 * rows), :], preferred_element_type=F32)
        own = dual_in[HALO + a, HALO : HALO + slices].astype(F32).reshape(slices * CH, bins)
        value = (own + value).astype(BF16).astype(F32)
        nd[a] = value
        for z in range(slices):
            cut[a, z : z + 1, :] = value[z * CH : z * CH + 1]

    def take(g, carry):
        found = []
        for a in range(angles):
            if groups > 1:
                select(HALO + a, g)
            found.append(
                lax.dot_general(
                    cut[a].astype(BF16), chosen[HALO + a], (((1,), (1,)), ((), ())), preferred_element_type=F32
                )
            )
        for t in range(batch):
            pieces[g * batch + t] = jnp.concatenate(
                [f[:, t * window : (t + 1) * window] for f in found], axis=1
            )
        return carry

    if groups == 1:
        take(0, 0)
    else:
        lax.fori_loop(0, groups, take, 0)

    def b_copy(k, row, target):
        return pltpu.make_async_remote_copy(
            src_ref=pieces.at[target],
            dst_ref=returned.at[row],
            send_sem=b_send.at[k - 1],
            recv_sem=b_recv.at[k - 1],
            device_id=(target, s),
            device_id_type=MESH,
        )

    for k in range(1, wide):
        b_copy(k, w, lax.rem(w + k, wide)).start()
    returned[w] = pieces[w]
    for z in range(slices):
        for c in range(mem):
            lines = [nd[a, z * CH + c : z * CH + c + 1, :] for a in range(angles)]
            dual_out[c, z] = jnp.concatenate(lines, axis=0).astype(BF16)
    for k in range(1, wide):
        b_copy(k, lax.rem(w + wide - k, wide), w).wait_recv()
    lines = jnp.concatenate([returned[t] for t in range(wide)], axis=1).astype(BF16)
    summed = lax.dot_general(lines, table[...], (((1,), (1,)), ((), ())), preferred_element_type=F32)
    back_out[...] = summed[:slices] * (1.0 / math.sqrt(angle_total))
    for k in range(1, wide):
        b_copy(k, w, lax.rem(w + k, wide)).wait_send()
    for i, j in p_moves:

        @pl.when(inside(w + i, s + j))
        def _():
            p_copy(i, j, s, (w, s)).wait_send()

    for i, j in d_moves:

        @pl.when(inside(w + i, s + j))
        def _():
            d_copy(i, j, (w, s)).wait_send()

    for k in range(1, wide):
        a_copy(k, w, lax.rem(w + k, wide)).wait_send()


def placed_band(flat, z, out_slices, block, same):
    width = flat.shape[1]
    by = ((z - 1 if same else z) * block) % width
    row = pltpu.roll(flat, by, axis=1) if by else flat
    lane = lax.broadcasted_iota(jnp.int32, (1, width), 1)
    if same and z == 0:
        row = jnp.where(lane < 2 * block, row, 0.0)
    if same and z == out_slices - 1:
        row = jnp.where(lane >= (z - 1) * block, row, 0.0)
    return row


def split_band(weights, stage, out, out_slices, same, o_pad):
    c_in, c_out = weights.shape[3:]
    block = 3 * c_in
    chunk = (out_slices if same else out_slices + 2) * block
    width = -(-chunk // 128) * 128
    held = -(-3 * block // 128) * 128
    assert width == chunk or not same
    for d1 in range(3):
        stage[...] = jnp.zeros_like(stage)
        for d0 in range(3):
            for d2 in range(3):
                at = (d0 * 3 + d2) * c_in
                stage[at : at + c_in, :c_out] = weights[d0, d1, d2].astype(F32)
        flat = stage[:held, :].T[:o_pad]
        if width > held:
            flat = jnp.concatenate([flat, jnp.zeros((o_pad, width - held), F32)], axis=1)
        for z in range(out_slices):
            row = placed_band(flat, z, out_slices, block, same)
            out[(d1 * out_slices + z) * o_pad : (d1 * out_slices + z + 1) * o_pad, :] = row[:, :chunk].astype(BF16)


def split_taps(weights, out, out_slices, same):
    c_out, _, c_in = weights.shape[2:]
    width = (out_slices if same else out_slices + 2) * c_in
    held = -(-width // 128) * 128
    assert width == held or not same
    for d1 in range(3):
        for d2 in range(3):
            lines = [weights[d0, d1, :, d2, :].astype(F32) for d0 in range(3)]
            flat = jnp.concatenate(lines + [jnp.zeros((c_out, held - 3 * c_in), F32)], axis=1)
            flat = jnp.concatenate([flat, jnp.zeros((CH - c_out, held), F32)], axis=0)
            rows = [placed_band(flat, z, out_slices, c_in, same) for z in range(out_slices)]
            at = (d1 * 3 + d2) * out_slices * CH
            out[at : at + out_slices * CH, :] = jnp.concatenate(rows, axis=0)[:, :width].astype(BF16)


def block_kernel(
    wide, slab, *refs
):
    given = refs[:12]
    vol_out, dual_out, back_out = refs[12:15]
    held, in_sem = refs[15:27], refs[27]
    volume, back_proj, dual_state, sinogram, offsets, p1, p2, p3, d1_w, d2_w, d3_w, trig = held
    (
        psrc, dsrc, frame, stack, arrived, windows, table, stage, pw1, pw2, pw3, dw1, dw2, dw3,
        px1, px2, px3, nv, deck, proj, x1, x2, x3, mine_out, cut_out, mine_in, cut_in, begins, wproj, xproj, base,
        p_send, p_recv, d_send, d_recv, e_send, e_recv, a_send, a_recv, b_send, b_recv,
    ) = refs[28:]
    w = lax.axis_index("wide")
    s = lax.axis_index("slab")
    mem, slices, pixels = volume.shape
    angles, bins = dual_state.shape[2:]
    angle_total = angles * wide
    depth = slices * slab
    edge = 4 * NY
    lanes = pixels + 2 * edge
    window = NY + 2 * TX
    hidden_channels = p1.shape[4]
    deep = slices + 2 * HALO
    reach_z, span_z = spans(slices)
    block = bins // wide
    broad = block + 128
    stride = block + 2 * MARGIN
    used = angle_total * stride
    total_lanes = deck.shape[1]

    def inside(i, j):
        return (i >= 0) & (i < wide) & (j >= 0) & (j < slab)

    loads = [pltpu.make_async_copy(src, dst, in_sem.at[n]) for n, (src, dst) in enumerate(zip(given, held))]
    for load in loads[:4]:
        load.start()
    frame[...] = jnp.zeros_like(frame)

    far = sorted(range(-(slab - 1), slab), key=lambda j: -abs(j))
    greet = [(i, j) for j in far for i in (0, -1, 1) if (i, j) != (0, 0)]
    barrier = pltpu.get_barrier_semaphore()
    total = jnp.int32(max(wide - 3, 0))
    for i, j in greet:
        there = inside(w + i, s + j)

        @pl.when(there)
        def _():
            pl.semaphore_signal(barrier, inc=1, device_id=(w + i, s + j), device_id_type=MESH)

        total = total + jnp.where(there, 1, 0)
    for k in range(2, wide - 1):
        pl.semaphore_signal(barrier, inc=1, device_id=(lax.rem(w + k, wide), s), device_id_type=MESH)
    if wide > 2:
        for end in (0, wide - 1):

            @pl.when(w == end)
            def _():
                pl.semaphore_signal(barrier, inc=1, device_id=(wide - 1 - end, s), device_id_type=MESH)

            total = total + jnp.where(w == end, 1, 0)

    for load in loads[:2]:
        load.wait()
    for z in range(slices):
        lines = [volume[c].astype(F32)[z : z + 1] for c in range(mem)]
        lines += [back_proj[z : z + 1, :], jnp.zeros((CH - mem - 1, pixels), F32)]
        psrc[z] = jnp.concatenate(lines, axis=0).astype(BF16)
    frame[pl.ds(s * slices, slices), :, edge : edge + pixels] = psrc[...]
    pl.semaphore_wait(barrier, total)

    def p_copy(i, j, row, target):
        if i == 0:
            src, dst = pl.ds(0, pixels), pl.ds(edge, pixels)
        elif i > 0:
            src, dst = pl.ds(pixels - edge, edge), pl.ds(0, edge)
        else:
            src, dst = pl.ds(0, edge), pl.ds(edge + pixels, edge)
        return pltpu.make_async_remote_copy(
            src_ref=psrc.at[:, :, src],
            dst_ref=frame.at[pl.ds(row * slices, slices), :, dst],
            send_sem=p_send.at[i + 1, j + slab - 1],
            recv_sem=p_recv.at[i + 1, j + slab - 1],
            device_id=target,
            device_id_type=MESH,
        )

    def d_copy(k, row, target):
        return pltpu.make_async_remote_copy(
            src_ref=dsrc.at[:, :, :, pl.ds(pl.multiple_of(target * block, 128), broad)],
            dst_ref=stack.at[pl.ds(row * angles, angles), pl.ds(HALO, slices)],
            send_sem=d_send.at[k - 1],
            recv_sem=d_recv.at[k - 1],
            device_id=(target, s),
            device_id_type=MESH,
        )

    def e_copy(j, target):
        z0, zn, zd = span_z[j]
        return pltpu.make_async_remote_copy(
            src_ref=stack.at[:, pl.ds(HALO + z0, zn)],
            dst_ref=stack.at[:, pl.ds(zd, zn)],
            send_sem=e_send.at[j + reach_z],
            recv_sem=e_recv.at[j + reach_z],
            device_id=(w, target),
            device_id_type=MESH,
        )

    p_moves = greet
    e_moves = [j for j in span_z if j != 0]
    for i, j in p_moves:

        @pl.when(inside(w + i, s + j))
        def _():
            p_copy(i, j, s, (w + i, s + j)).start()

    for load in loads[2:4]:
        load.wait()
    for z in range(slices):
        for a in range(angles):
            lines = [dual_state[c, z].astype(F32)[a : a + 1] for c in range(mem)]
            lines += [jnp.zeros((1, bins), F32), sinogram[z].astype(F32)[a : a + 1]]
            lines += [jnp.zeros((CH - mem - 2, bins), F32)]
            line = jnp.concatenate([jnp.concatenate(lines, axis=0), jnp.zeros((CH, 128), F32)], axis=1)
            dsrc[a, z] = pltpu.roll(line, 64, axis=1).astype(BF16)
    for k in range(1, wide):
        d_copy(k, w, lax.rem(w + k, wide)).start()
    for load in loads[4:]:
        load.start()
    stack[pl.ds(w * angles, angles), HALO : HALO + slices] = dsrc[
        :, :, :, pl.ds(pl.multiple_of(w * block, 128), broad)
    ]
    deck[...] = jnp.zeros_like(deck)
    proj[...] = jnp.zeros_like(proj)
    for load in loads[4:]:
        load.wait()
    build_band(p1, stage, pw1, depth, True, CH, 4, hidden_channels)
    split_band(p2, stage, pw2, depth, True, hidden_channels)
    split_taps(p3, pw3, depth, True)
    begin_columns = offsets[...]
    for a in range(angle_total):
        begins[a] = jnp.broadcast_to(begin_columns[:, a : a + 1], (wide, 128))
    per = 128 // window
    part_of = lax.broadcasted_iota(jnp.int32, (1, 128), 1) // window
    detector = []
    for first in range(0, angle_total, per):
        own = begins[first, pl.ds(w, 1), :]
        for n in range(1, per):
            own = jnp.where(part_of == n, begins[first + n, pl.ds(w, 1), :], own)
        detector.append((lax.broadcasted_iota(jnp.int32, (1, 128), 1) - own) & (window - 1))
    build_table(trig, table, jnp.concatenate(detector, axis=1).astype(F32))
    build_band(d1_w, stage, dw1, deep - 2, False, CH, 4, hidden_channels)
    choice = lax.broadcasted_iota(jnp.int32, (1, wproj.shape[1]), 1)
    chosen_row = jnp.full_like(choice, -1)
    for d1 in range(3):
        for d2 in range(3):
            first = (d1 * 3 + d2) * deep
            here = (choice >= first) & (choice < first + deep)
            chosen_row = jnp.where(here, ((choice - first + d1 * deep) * 4 + d2) * CH + mem, chosen_row)
    picked = lax.broadcasted_iota(jnp.int32, (dw1.shape[1], wproj.shape[1]), 0) == chosen_row
    picked = jnp.where(picked, 1.0, 0.0).astype(BF16)
    wproj[...] = jnp.dot(dw1[...], picked, preferred_element_type=F32).astype(BF16)
    split_band(d2_w, stage, dw2, deep - 4, False, hidden_channels)
    split_taps(d3_w, dw3, slices, False)
    for k in range(1, wide):
        d_copy(k, lax.rem(w + wide - k, wide), w).wait_recv()
    for j in e_moves:

        @pl.when(inside(w, s + j))
        def _():
            e_copy(j, s + j).start()

    for i, j in p_moves:

        @pl.when(inside(w - i, s - j))
        def _():
            p_copy(i, j, s - j, (w, s)).wait_recv()


    plane = lax.broadcasted_iota(jnp.int32, (1, lanes), 1)
    y = plane % NY
    x = w * TX + plane // NY - 4
    grid_mask = (x >= 0) & (x < wide * TX)
    y_mask = {-1: y > 0, 0: None, 1: y < NY - 1}

    def tap(value, d1, d2):
        moved = shifted(value, NY * d1 + d2)
        return moved if d2 == 0 else jnp.where(y_mask[d2], moved, 0.0)

    field = frame[...].astype(F32)
    pblank = jnp.zeros((CH, lanes), F32)
    for z in range(depth):
        for d1 in range(3):
            parts = [tap(field[z], d1 - 1, d2) for d2 in (-1, 0, 1)] + [pblank]
            px1[pl.ds((d1 * depth + z) * 4 * CH, 4 * CH), :] = jnp.concatenate(parts, axis=0).astype(BF16)

    def within(value):
        return jnp.where(grid_mask, jnp.maximum(value, 0.0), 0.0)

    hid = hidden_channels
    value = within(jnp.dot(pw1[...], px1[...], preferred_element_type=F32))
    for d2 in range(3):
        moved = tap(value, 0, d2 - 1).astype(BF16)
        for z in range(depth):
            px2[(z * 3 + d2) * hid : (z * 3 + d2 + 1) * hid, :] = moved[z * hid : (z + 1) * hid]
    rows = depth * hid
    value = jnp.dot(pw2[rows : 2 * rows, :], px2[...], preferred_element_type=F32)
    for d1 in (0, 2):
        part = jnp.dot(pw2[d1 * rows : (d1 + 1) * rows, :], px2[...], preferred_element_type=F32)
        value = value + shifted(part, (d1 - 1) * NY)
    px3[...] = within(value).astype(BF16)
    part = jnp.dot(pw3[...], px3[...], preferred_element_type=F32)
    rows = depth * CH
    three = jnp.zeros((rows, lanes), F32)
    for d1 in range(3):
        for d2 in range(3):
            n = d1 * 3 + d2
            three = three + tap(part[n * rows : (n + 1) * rows], d1 - 1, d2 - 1)
    updated = field.reshape(depth * CH, lanes) + three
    updated = updated[:, edge : edge + pixels].astype(BF16).astype(F32)
    nv[...] = updated.reshape(depth, CH, pixels)
    leading = jnp.concatenate([updated[z * CH : z * CH + 1] for z in range(depth)], axis=0).astype(BF16)
    windows[...] = jnp.dot(leading, table[...], preferred_element_type=F32).astype(BF16)

    def a_copy(k, row, target):
        return pltpu.make_async_remote_copy(
            src_ref=windows,
            dst_ref=arrived.at[row],
            send_sem=a_send.at[k - 1],
            recv_sem=a_recv.at[k - 1],
            device_id=(target, s),
            device_id_type=MESH,
        )

    for k in range(1, wide):
        a_copy(k, w, lax.rem(w + k, wide)).start()
    arrived[w] = windows[...]

    mine = [nv[s * slices + z] for z in range(slices)]
    for c in range(mem):
        vol_out[c] = jnp.concatenate([m[c : c + 1] for m in mine], axis=0).astype(BF16)
    for j in e_moves:

        @pl.when(inside(w, s - j))
        def _():
            e_copy(j, s).wait_recv()

    skip = 64 - MARGIN
    for a in range(angle_total):
        for z in range(deep):
            value = stack[a, z].astype(F32)[:, skip : skip + stride]
            if z < HALO or z >= HALO + slices:
                row_z = s * slices + z - HALO
                value = jnp.where((row_z >= 0) & (row_z < depth), value, 0.0)
            deck[z * CH : (z + 1) * CH, a * stride : (a + 1) * stride] = value
    lane = lax.broadcasted_iota(jnp.int32, (1, total_lanes), 1)
    begin = jnp.zeros_like(lane)
    for a in range(1, angle_total):
        begin = jnp.where(lane >= a * stride, a * stride, begin)
    bin_at = w * block - MARGIN + lane - begin
    lane_ok = (lane < used) & (bin_at >= 0) & (bin_at < bins)
    blank = jnp.zeros((CH, total_lanes), F32)
    for z in range(deep):
        value = deck[z * CH : (z + 1) * CH, :]
        for d1 in range(3):
            parts = [shifted(value, (d1 - 1) * stride + d2 - 1) for d2 in range(3)] + [blank]
            x1[(d1 * deep + z) * 4 * CH : (d1 * deep + z + 1) * 4 * CH, :] = jnp.concatenate(parts, axis=0).astype(BF16)
    base[...] = jnp.dot(dw1[...], x1[...], preferred_element_type=F32)
    for k in range(1, wide):
        a_copy(k, lax.rem(w + wide - k, wide), w).wait_recv()

    at = lax.broadcasted_iota(jnp.int32, (depth, 128), 1)
    bins_at = [at + (w * block - 64 + n * 128) for n in range(broad // 128)]
    for first in range(0, angle_total, per):
        placed = [[jnp.zeros((depth, 128), F32) for _ in bins_at] for _ in range(per)]
        for t in range(wide):
            source = arrived[t, :, first * window : first * window + 128].astype(F32)
            for n in range(per):
                line = source
                for m in range(per):
                    if m != n:
                        line = jnp.where(at // window == m, pltpu.roll(source, (m - n) * window % 128, axis=1), line)
                begin = begins[first + n, t : t + 1, :]
                for m, bin_of in enumerate(bins_at):
                    inner = bin_of - begin
                    placed[n][m] = placed[n][m] + jnp.where((inner >= 0) & (inner < window), line, 0.0)
        for n in range(per):
            line = jnp.concatenate(placed[n], axis=1) * (1.0 / math.sqrt(NY))
            line = line.astype(BF16).astype(F32)[:, skip : skip + stride]
            proj[8 : 8 + depth, (first + n) * stride : (first + n + 1) * stride] = line

    def kept(value, out_slices, margin):
        hid = value.shape[0] // out_slices
        row_z = s * slices - margin + lax.broadcasted_iota(jnp.int32, (value.shape[0], 1), 0) // hid
        return jnp.where((row_z >= 0) & (row_z < depth) & lane_ok, jnp.maximum(value, 0.0), 0.0)

    line = jnp.concatenate([proj[pl.ds(8 - HALO + s * slices + z, 1), :] for z in range(deep)], axis=0)
    parts = [shifted(line, (d1 - 1) * stride + d2 - 1) for d1 in range(3) for d2 in range(3)]
    parts += [jnp.zeros((xproj.shape[0] - 9 * deep, total_lanes), F32)]
    xproj[...] = jnp.concatenate(parts, axis=0).astype(BF16)
    hid = hidden_channels
    value = base[...] + jnp.dot(wproj[...], xproj[...], preferred_element_type=F32)
    value = kept(value, deep - 2, 2)
    for d2 in range(3):
        moved = shifted(value, d2 - 1).astype(BF16)
        for z in range(deep - 2):
            x2[(z * 3 + d2) * hid : (z * 3 + d2 + 1) * hid, :] = moved[z * hid : (z + 1) * hid]
    rows = (deep - 4) * hid
    value = jnp.zeros((rows, total_lanes), F32)
    for d1 in range(3):
        part = jnp.dot(dw2[d1 * rows : (d1 + 1) * rows, :], x2[...], preferred_element_type=F32)
        value = value + shifted(part, (d1 - 1) * stride)
    x3[...] = kept(value, deep - 4, 1).astype(BF16)
    part = jnp.dot(dw3[...], x3[...], preferred_element_type=F32)
    rows = slices * CH
    value = deck[HALO * CH : HALO * CH + rows, :]
    for d1 in range(3):
        for d2 in range(3):
            n = d1 * 3 + d2
            value = value + shifted(part[n * rows : (n + 1) * rows], (d1 - 1) * stride + d2 - 1)
    value = value.astype(BF16).astype(F32)
    heads = []
    for a in range(angle_total):
        own = value[:, a * stride + MARGIN : a * stride + MARGIN + block]
        mine_out[a] = own.astype(BF16)
        heads += [own[z * CH : z * CH + 1] for z in range(slices)]
    cut_out[...] = jnp.concatenate(heads, axis=0).astype(BF16)

    def b_copy(n, k, row, target):
        lanes_of = pl.ds(pl.multiple_of(row * block, 128), block)
        if n == 0:
            src, dst = cut_out, cut_in.at[:, lanes_of]
        else:
            src, dst = mine_out.at[pl.ds(target * angles, angles)], mine_in.at[:, :, lanes_of]
        return pltpu.make_async_remote_copy(
            src_ref=src,
            dst_ref=dst,
            send_sem=b_send.at[n, k - 1],
            recv_sem=b_recv.at[n, k - 1],
            device_id=(target, s),
            device_id_type=MESH,
        )

    for n in range(2):
        for k in range(1, wide):
            b_copy(n, k, w, lax.rem(w + k, wide)).start()
    lanes_of = pl.ds(pl.multiple_of(w * block, 128), block)
    cut_in[:, lanes_of] = cut_out[...]
    mine_in[:, :, lanes_of] = mine_out[pl.ds(w * angles, angles)]
    for i, j in p_moves:

        @pl.when(inside(w + i, s + j))
        def _():
            p_copy(i, j, s, (w, s)).wait_send()

    for k in range(1, wide):
        d_copy(k, w, lax.rem(w + k, wide)).wait_send()
    for j in e_moves:

        @pl.when(inside(w, s + j))
        def _():
            e_copy(j, s + j).wait_send()

    for k in range(1, wide):
        a_copy(k, w, lax.rem(w + k, wide)).wait_send()
    for n in range(2):
        for k in range(1, wide):
            b_copy(n, k, w, lax.rem(w + k, wide)).wait_send()
    for k in range(1, wide):
        b_copy(0, k, lax.rem(w + wide - k, wide), w).wait_recv()
    line8 = lax.broadcasted_iota(jnp.int32, (8, 128), 0)
    lane8 = lax.broadcasted_iota(jnp.int32, (8, 128), 1)
    cut = cut_in[...].astype(F32)
    taken = []
    for first in range(0, angle_total, per):
        joined = jnp.zeros((8, 128), F32)
        for n in range(per):
            a = first + n
            begin = begins[a, pl.ds(w, 1), :]
            group = a * slices // 8 * 8
            found = jnp.zeros((8, 128), F32)
            for m in range(0, bins, 128):
                inner = lane8 + m - begin
                found = jnp.where((inner >= 0) & (inner < window), cut[group : group + 8, m : m + 128], found)
            both = found
            for m in range(1, per):
                both = both + pltpu.roll(found, m * window, axis=1)
            at_row = a * slices - group
            here = (lane8 // window == n) & (line8 >= at_row) & (line8 < at_row + slices)
            joined = jnp.where(here, both, joined)
        taken.append(joined)
    lines = jnp.concatenate(taken, axis=1).astype(BF16)
    summed = lax.dot_general(lines, table[...], (((1,), (1,)), ((), ())), preferred_element_type=F32)
    total_back = summed[:slices]
    for n in range(1, 8 // slices):
        total_back = total_back + summed[n * slices : (n + 1) * slices]
    back_out[...] = total_back * (1.0 / math.sqrt(angle_total))
    for k in range(1, wide):
        b_copy(1, k, lax.rem(w + wide - k, wide), w).wait_recv()
    for z in range(slices):
        for c in range(mem):
            lines = [mine_in[a].astype(F32)[z * CH + c : z * CH + c + 1] for a in range(angles)]
            dual_out[c, z] = jnp.concatenate(lines, axis=0).astype(BF16)


def hand_on(outs):
    def kernel(*refs):
        for src, dst in zip(refs[:3], refs[3:]):
            dst[...] = src[...]

    space = pl.BlockSpec(memory_space=pltpu.VMEM)
    return pl.pallas_call(
        kernel,
        out_shape=tuple(jax.ShapeDtypeStruct(o.shape, o.dtype) for o in outs),
        in_specs=[space] * 3,
        out_specs=(space,) * 3,
        name="hand_on",
    )(*outs)


def block_body(wide, slab, volume, back_proj, dual_state, sinogram, offsets, p1, p2, p3, d1, d2, d3):
    mem, slices, pixels = volume.shape
    angles, bins = dual_state.shape[2:]
    depth = slices * slab
    angle_total = angles * wide
    hidden = p1.shape[4]
    reach_z, _ = spans(slices)
    lanes = pixels + 8 * NY
    window = NY + 2 * TX
    block = bins // wide
    stride = block + 2 * MARGIN
    spread_lanes = -(-((angle_total + 1) * stride + 1) // 128) * 128
    deep = slices + 2 * HALO
    dma = pltpu.SemaphoreType.DMA
    vmem = pltpu.VMEM
    space = pl.BlockSpec(memory_space=pltpu.VMEM)
    args = (volume, back_proj, dual_state, sinogram, offsets, p1, p2, p3.transpose(0, 1, 4, 2, 3))
    args += (d1, d2, d3.transpose(0, 1, 4, 2, 3), jnp.asarray(trig_rows(angle_total)))
    outs = pl.pallas_call(
        functools.partial(block_kernel, wide, slab),
        out_shape=(
            jax.ShapeDtypeStruct(volume.shape, BF16),
            jax.ShapeDtypeStruct(dual_state.shape, BF16),
            jax.ShapeDtypeStruct(back_proj.shape, F32),
        ),
        in_specs=[pl.BlockSpec(memory_space=pl.ANY)] * 12,
        out_specs=(space,) * 3,
        scratch_shapes=[vmem(a.shape, a.dtype) for a in args]
        + [dma((12,))]
        + [
            vmem((slices, CH, pixels), BF16),
            vmem((angles, slices, CH, bins + 128), BF16),
            vmem((depth, CH, lanes), BF16),
            vmem((angle_total, deep, CH, block + 128), BF16),
            vmem((wide, depth, angle_total * window), BF16),
            vmem((depth, angle_total * window), BF16),
            vmem((pixels, angle_total * window), BF16),
            vmem((-(-9 * hidden // 128) * 128, 128), F32),
            vmem((depth * hidden, 12 * depth * CH), BF16),
            vmem((3 * depth * hidden, 3 * depth * hidden), BF16),
            vmem((9 * depth * CH, depth * hidden), BF16),
            vmem(((deep - 2) * hidden, 12 * deep * CH), BF16),
            vmem((3 * (deep - 4) * hidden, 3 * (deep - 2) * hidden), BF16),
            vmem((9 * slices * CH, (deep - 4) * hidden), BF16),
            vmem((12 * depth * CH, lanes), BF16),
            vmem((3 * depth * hidden, lanes), BF16),
            vmem((depth * hidden, lanes), BF16),
            vmem((depth, CH, pixels), F32),
            vmem((deep * CH, spread_lanes), F32),
            vmem((-(-depth // 8) * 8 + 16, spread_lanes), F32),
            vmem((12 * deep * CH, spread_lanes), BF16),
            vmem((3 * (deep - 2) * hidden, spread_lanes), BF16),
            vmem(((deep - 4) * hidden, spread_lanes), BF16),
            vmem((angle_total, slices * CH, block), BF16),
            vmem((angle_total * slices, block), BF16),
            vmem((angles, slices * CH, bins), BF16),
            vmem((angle_total * slices, bins), BF16),
            vmem((angle_total, wide, 128), jnp.int32),
            vmem(((deep - 2) * hidden, -(-9 * deep // 16) * 16), BF16),
            vmem((-(-9 * deep // 16) * 16, spread_lanes), BF16),
            vmem(((deep - 2) * hidden, spread_lanes), F32),
            dma((3, 2 * slab - 1)),
            dma((3, 2 * slab - 1)),
            dma((wide - 1,)),
            dma((wide - 1,)),
            dma((2 * reach_z + 1,)),
            dma((2 * reach_z + 1,)),
            dma((wide - 1,)),
            dma((wide - 1,)),
            dma((2, wide - 1)),
            dma((2, wide - 1)),
        ],
        compiler_params=pltpu.CompilerParams(
            collective_id=0, has_side_effects=True, vmem_limit_bytes=VMEM_LIMIT
        ),
        name="block_kernel",
    )(*args)
    return hand_on(outs)


def body(wide, slab, volume, back_proj, dual_state, sinogram, offsets, p1, p2, p3, d1, d2, d3):
    mem, slices, pixels = volume.shape
    angles, bins = dual_state.shape[2:]
    if bins % (128 * wide) == 0 and 8 % slices == 0 and (slices + 2 * HALO) % 8 == 0 and angles * wide * slices % 16 == 0:
        return block_body(wide, slab, volume, back_proj, dual_state, sinogram, offsets, p1, p2, p3, d1, d2, d3)
    depth = slices * slab
    angle_total = angles * wide
    hidden = p1.shape[4]
    group = angles * (NY + 2 * TX)
    reach_a, _ = spans(angles)
    reach_z, _ = spans(slices)
    lanes = pixels + 8 * NY
    wide_angles = angles + 2 * HALO
    deep = slices + 2 * HALO
    dma = pltpu.SemaphoreType.DMA
    vmem = pltpu.VMEM
    space = pl.BlockSpec(memory_space=pltpu.VMEM)
    args = (volume, back_proj, dual_state, sinogram, offsets, p1, p2, p3.transpose(0, 1, 4, 2, 3))
    args += (d1, d2, d3.transpose(0, 1, 4, 2, 3), jnp.asarray(trig_rows(angle_total)))
    outs = pl.pallas_call(
        functools.partial(whole_kernel, wide, slab),
        out_shape=(
            jax.ShapeDtypeStruct(volume.shape, BF16),
            jax.ShapeDtypeStruct(dual_state.shape, BF16),
            jax.ShapeDtypeStruct(back_proj.shape, F32),
        ),
        in_specs=[pl.BlockSpec(memory_space=pl.ANY)] * 12,
        out_specs=(space,) * 3,
        scratch_shapes=[vmem(a.shape, a.dtype) for a in args]
        + [dma((12,))]
        + [
            vmem((slices, CH, pixels), BF16),
            vmem((angles, slices, CH, bins), BF16),
            vmem((depth, CH, lanes), BF16),
            vmem((wide_angles, deep, CH, bins), BF16),
            vmem((wide, depth, (2 * reach_a + 1) * group), BF16),
            vmem((depth, (wide + 2 * reach_a) * group), BF16),
            vmem((pixels, angle_total * (NY + 2 * TX)), BF16),
            vmem((-(-9 * hidden // 128) * 128, 128), F32),
            vmem((depth * hidden, 12 * depth * CH), BF16),
            vmem((depth * hidden, 9 * depth * hidden), BF16),
            vmem((depth * CH, 9 * depth * hidden), BF16),
            vmem(((deep - 2) * hidden, 12 * deep * CH), BF16),
            vmem(((deep - 4) * hidden, 9 * (deep - 2) * hidden), BF16),
            vmem(((deep - 6) * CH, 9 * (deep - 4) * hidden), BF16),
            vmem((12 * depth * CH, lanes), BF16),
            vmem((9 * depth * hidden, lanes), BF16),
            vmem((depth, CH, pixels), F32),
            vmem((wide_angles, math.gcd(wide, 8) * (NY + 2 * TX), bins), BF16),
            vmem((depth + 2 * HALO, wide_angles, bins), F32),
            vmem((wide_angles * deep * 4 * CH, bins), BF16),
            vmem(((wide_angles - 2) * (deep - 2) * 3 * hidden, bins), BF16),
            vmem(((wide_angles - 4) * (deep - 4) * 3 * hidden, bins), BF16),
            vmem((angles, slices * CH, bins), F32),
            vmem((angles, 8, bins), F32),
            vmem((wide, 8, group), F32),
            vmem((wide, 8, group), F32),
            dma((3, 2 * slab - 1)),
            dma((3, 2 * slab - 1)),
            dma((2 * reach_a + 1, 2 * reach_z + 1)),
            dma((2 * reach_a + 1, 2 * reach_z + 1)),
            dma((wide - 1,)),
            dma((wide - 1,)),
            dma((wide - 1,)),
            dma((wide - 1,)),
        ],
        compiler_params=pltpu.CompilerParams(
            collective_id=0, has_side_effects=True, vmem_limit_bytes=VMEM_LIMIT
        ),
        name="whole_kernel",
    )(*args)
    return hand_on(outs)


def solution(mesh):
    wide, slab = mesh.shape["wide"], mesh.shape["slab"]
    in_specs = (
        P(None, "slab", "wide"),
        P("slab", "wide"),
        P(None, "slab", "wide", None),
        P("slab", "wide", None),
    ) + (P(),) * 7
    out_specs = (P(None, "slab", "wide"), P(None, "slab", "wide", None), P("slab", "wide"))
    return jax.shard_map(
        functools.partial(body, wide, slab), mesh=mesh, in_specs=in_specs, out_specs=out_specs, check_vma=False
    )
```

```python
import functools
import math

import jax
import jax.numpy as jnp
import numpy as np
from jax import lax
from jax.experimental import pallas as pl
from jax.experimental.pallas import tpu as pltpu
from jax.sharding import PartitionSpec as P

NY = 32
TX = 16
HALO = 3
CH = 8
MARGIN = HALO
MESH = pl.DeviceIdType.MESH
F32 = jnp.float32
BF16 = jnp.bfloat16
VMEM_LIMIT = 60 * 1024 * 1024


def trig_rows(angle_total):
    window = NY + 2 * TX
    angle = np.arange(angle_total, dtype=np.float32) * np.float32(math.pi / angle_total)
    rows = np.zeros((8, angle_total * window), np.float32)
    rows[0] = np.repeat(np.cos(angle), window)
    rows[1] = np.repeat(np.sin(angle), window)
    rows[2] = np.tile(np.arange(window, dtype=np.float32), angle_total)
    return rows


def build_table(trig, table, detector=None):
    cosine, sine = trig[0:1, :], trig[1:2, :]
    detector = trig[2:3, :] if detector is None else detector
    centre_y = lax.broadcasted_iota(jnp.int32, (NY, trig.shape[1]), 0).astype(F32) - (NY - 1) / 2.0

    def row(i, carry):
        centre_x = lax.convert_element_type(i, F32) - (TX - 1) / 2.0
        positions = centre_x * cosine + centre_y * sine + (NY + 2 * TX) / 2.0
        value = jnp.maximum(0.0, 1.0 - jnp.abs(positions - detector))
        table[pl.ds(pl.multiple_of(i * NY, NY), NY), :] = value.astype(BF16)
        return carry

    lax.fori_loop(0, TX, row, 0)


def build_band(weights, stage, out, out_slices, same, c_pad, bin_pad, o_pad, turn=False):
    if turn:
        c_out, _, c_in = weights.shape[2:]
    else:
        c_in, c_out = weights.shape[3:]
    block = bin_pad * c_pad
    in_slices = out_slices if same else out_slices + 2
    chunk = in_slices * block
    width = chunk if chunk % 128 == 0 else -(-3 * chunk // 128) * 128
    held = -(-3 * block // 128) * 128
    pieces = []
    for d1 in range(3):
        if turn:
            lines = []
            for d0 in range(3):
                lines += [weights[d0, d1, :, d2, :].astype(F32) for d2 in range(3)]
            flat = jnp.concatenate(lines + [jnp.zeros((c_out, held - 9 * c_in), F32)], axis=1)
            flat = jnp.concatenate([flat, jnp.zeros((o_pad - c_out, held), F32)], axis=0)
        else:
            stage[...] = jnp.zeros_like(stage)
            for d0 in range(3):
                for d2 in range(3):
                    at = (d0 * bin_pad + d2) * c_pad
                    stage[at : at + c_in, :c_out] = weights[d0, d1, d2].astype(F32)
            flat = stage[:held, :].T[:o_pad]
        if width > held:
            flat = jnp.concatenate([flat, jnp.zeros((o_pad, width - held), F32)], axis=1)
        pieces.append(flat[:, :width])
    lane = lax.broadcasted_iota(jnp.int32, (1, width), 1)

    def turned(piece, by):
        by = by % width
        return pltpu.roll(piece, by, axis=1) if by else piece

    waiting = []
    for z in range(out_slices):
        if chunk % 128 == 0:
            parts = []
            for piece in pieces:
                part = turned(piece, (z - 1 if same else z) * block)
                if same and z == 0:
                    part = jnp.where(lane < 2 * block, part, 0.0)
                if same and z == out_slices - 1:
                    part = jnp.where(lane >= (z - 1) * block, part, 0.0)
                parts.append(part)
            row = jnp.concatenate(parts, axis=1)
        else:
            assert not same
            row = sum(turned(piece, d1 * chunk + z * block) for d1, piece in enumerate(pieces))
        waiting.append(row)
        rows = len(waiting) * o_pad
        if rows % 16 == 0:
            both = waiting[0] if len(waiting) == 1 else jnp.concatenate(waiting, axis=0)
            out[(z + 1) * o_pad - rows : (z + 1) * o_pad, :] = both[:, : 3 * chunk].astype(BF16)
            waiting = []
    assert not waiting


def shifted(value, by):
    lanes = value.shape[-1]
    return value if by == 0 else pltpu.roll(value, (-by) % lanes, axis=value.ndim - 1)


def spans(block):
    reach = -(-HALO // block)
    result = {}
    for d in range(-reach, reach + 1):
        count = block if d == 0 else min(block, HALO - (abs(d) - 1) * block)
        first = block - count if d > 0 else 0
        result[d] = (first, count, first - d * block + HALO)
    return reach, result


def whole_kernel(
    wide, slab, *refs
):
    given = refs[:12]
    vol_out, dual_out, back_out = refs[12:15]
    held, in_sem = refs[15:27], refs[27]
    volume, back_proj, dual_state, sinogram, offsets, p1, p2, p3, d1_w, d2_w, d3_w, trig = held
    (
    psrc, dsrc, frame, dual_in, arrived, wsend, table, stage, pw1, pw2, pw3, dw1, dw2, dw3,
    px1, px2, nv, chosen, proj, x1, x2, x3, nd, cut, pieces, returned,
    p_send, p_recv, d_send, d_recv, a_send, a_recv, b_send, b_recv,
    ) = refs[28:]
    w = lax.axis_index("wide")
    s = lax.axis_index("slab")
    mem, slices, pixels = volume.shape
    angles, bins = dual_state.shape[2:]
    angle_total = angles * wide
    depth = slices * slab
    edge = 4 * NY
    lanes = pixels + 2 * edge
    window = NY + 2 * TX
    hidden_channels = p1.shape[4]
    wide_angles = angles + 2 * HALO
    deep = slices + 2 * HALO
    reach_a, span_a = spans(angles)
    reach_z, span_z = spans(slices)
    group = angles * window
    cover = (2 * reach_a + 1) * group

    def inside(i, j):
        return (i >= 0) & (i < wide) & (j >= 0) & (j < slab)

    frame[...] = jnp.zeros_like(frame)
    dual_in[...] = jnp.zeros_like(dual_in)

    reach_w = max(1, reach_a)
    greet = [
        (i, j) for i in range(-reach_w, reach_w + 1) for j in range(-(slab - 1), slab) if (i, j) != (0, 0)
    ]
    barrier = pltpu.get_barrier_semaphore()
    total = jnp.int32(wide - 1)
    for i, j in greet:
        there = inside(w + i, s + j)

        @pl.when(there)
        def _():
            pl.semaphore_signal(barrier, inc=1, device_id=(w + i, s + j), device_id_type=MESH)

        total = total + jnp.where(there, 1, 0)
    for k in range(1, wide):
        pl.semaphore_signal(barrier, inc=1, device_id=(lax.rem(w + k, wide), s), device_id_type=MESH)

    loads = [pltpu.make_async_copy(src, dst, in_sem.at[n]) for n, (src, dst) in enumerate(zip(given, held))]
    for load in loads:
        load.start()
    wsend[...] = jnp.zeros_like(wsend)
    for load in loads[:4]:
        load.wait()
    for z in range(slices):
        lines = [volume[c].astype(F32)[z : z + 1] for c in range(mem)]
        lines += [back_proj[z : z + 1, :], jnp.zeros((CH - mem - 1, pixels), F32)]
        psrc[z] = jnp.concatenate(lines, axis=0).astype(BF16)
        for a in range(angles):
            lines = [dual_state[c, z].astype(F32)[a : a + 1] for c in range(mem)]
            lines += [jnp.zeros((1, bins), F32), sinogram[z].astype(F32)[a : a + 1]]
            lines += [jnp.zeros((CH - mem - 2, bins), F32)]
            dsrc[a, z] = jnp.concatenate(lines, axis=0).astype(BF16)
    frame[pl.ds(s * slices, slices), :, edge : edge + pixels] = psrc[...]
    dual_in[HALO : HALO + angles, HALO : HALO + slices] = dsrc[...]
    pl.semaphore_wait(barrier, total)

    def p_copy(i, j, row, target):
        if i == 0:
            src, dst = pl.ds(0, pixels), pl.ds(edge, pixels)
        elif i > 0:
            src, dst = pl.ds(pixels - edge, edge), pl.ds(0, edge)
        else:
            src, dst = pl.ds(0, edge), pl.ds(edge + pixels, edge)
        return pltpu.make_async_remote_copy(
            src_ref=psrc.at[:, :, src],
            dst_ref=frame.at[pl.ds(row * slices, slices), :, dst],
            send_sem=p_send.at[i + 1, j + slab - 1],
            recv_sem=p_recv.at[i + 1, j + slab - 1],
            device_id=target,
            device_id_type=MESH,
        )

    def d_copy(i, j, target):
        a0, an, ad = span_a[i]
        z0, zn, zd = span_z[j]
        return pltpu.make_async_remote_copy(
            src_ref=dsrc.at[pl.ds(a0, an), pl.ds(z0, zn)],
            dst_ref=dual_in.at[pl.ds(ad, an), pl.ds(zd, zn)],
            send_sem=d_send.at[i + reach_a, j + reach_z],
            recv_sem=d_recv.at[i + reach_a, j + reach_z],
            device_id=target,
            device_id_type=MESH,
        )

    p_moves = [(i, j) for i in (-1, 0, 1) for j in range(-(slab - 1), slab) if (i, j) != (0, 0)]
    d_moves = [(i, j) for i in span_a for j in span_z if (i, j) != (0, 0)]
    for i, j in p_moves:

        @pl.when(inside(w + i, s + j))
        def _():
            p_copy(i, j, s, (w + i, s + j)).start()

    for i, j in d_moves:

        @pl.when(inside(w + i, s + j))
        def _():
            d_copy(i, j, (w + i, s + j)).start()


    for load in loads[4:]:
        load.wait()
    batch = math.gcd(wide, 8)
    groups = wide // batch
    relative = lax.broadcasted_iota(jnp.int32, (window, bins), 1) - lax.broadcasted_iota(
        jnp.int32, (window, bins), 0
    )

    def select(a, g):
        column = jnp.clip(w * angles + a - HALO, 0, angle_total - 1)
        rows = offsets[pl.ds(g * batch, batch), :]
        here = lax.broadcasted_iota(jnp.int32, rows.shape, 1) == column
        begin = jnp.sum(jnp.where(here, rows, 0), axis=1, keepdims=True)
        for t in range(batch):
            hit = relative == begin[t : t + 1]
            chosen[a, t * window : (t + 1) * window, :] = jnp.where(hit, 1.0, 0.0).astype(BF16)

    build_band(p1, stage, pw1, depth, True, CH, 4, hidden_channels)
    build_band(p2, stage, pw2, depth, True, hidden_channels, 3, hidden_channels)
    build_band(p3, stage, pw3, depth, True, hidden_channels, 3, CH, True)
    build_table(trig, table)
    build_band(d1_w, stage, dw1, deep - 2, False, CH, 4, hidden_channels)
    build_band(d2_w, stage, dw2, deep - 4, False, hidden_channels, 3, hidden_channels)
    build_band(d3_w, stage, dw3, deep - 6, False, hidden_channels, 3, CH, True)
    if groups == 1:
        for a in range(wide_angles):
            select(a, 0)

    for i, j in p_moves:

        @pl.when(inside(w - i, s - j))
        def _():
            p_copy(i, j, s - j, (w, s)).wait_recv()


    plane = lax.broadcasted_iota(jnp.int32, (1, lanes), 1)
    y = plane % NY
    x = w * TX + plane // NY - 4
    grid_mask = (x >= 0) & (x < wide * TX)
    y_mask = {-1: y > 0, 0: None, 1: y < NY - 1}

    def tap(value, d1, d2):
        moved = shifted(value, NY * d1 + d2)
        return moved if d2 == 0 else jnp.where(y_mask[d2], moved, 0.0)

    field = frame[...].astype(F32)
    pblank = jnp.zeros((CH, lanes), F32)
    for z in range(depth):
        for d1 in range(3):
            parts = [tap(field[z], d1 - 1, d2) for d2 in (-1, 0, 1)] + [pblank]
            px1[pl.ds((d1 * depth + z) * 4 * CH, 4 * CH), :] = jnp.concatenate(parts, axis=0).astype(BF16)

    def spread(hidden):
        hid = hidden.shape[0] // depth
        for d1 in range(3):
            for d2 in range(3):
                moved = tap(hidden, d1 - 1, d2 - 1).astype(BF16)
                for z in range(depth):
                    px2[pl.ds(((d1 * depth + z) * 3 + d2) * hid, hid), :] = moved[z * hid : (z + 1) * hid]

    one = jnp.dot(pw1[...], px1[...], preferred_element_type=F32)
    spread(jnp.where(grid_mask, jnp.maximum(one, 0.0), 0.0))
    two = jnp.dot(pw2[...], px2[...], preferred_element_type=F32)
    spread(jnp.where(grid_mask, jnp.maximum(two, 0.0), 0.0))
    three = jnp.dot(pw3[...], px2[...], preferred_element_type=F32)
    updated = field.reshape(depth * CH, lanes) + three
    updated = updated[:, edge : edge + pixels].astype(BF16).astype(F32)
    nv[...] = updated.reshape(depth, CH, pixels)
    leading = jnp.concatenate([updated[z * CH : z * CH + 1] for z in range(depth)], axis=0).astype(BF16)
    windows = jnp.dot(leading, table[...], preferred_element_type=F32).astype(BF16)
    wsend[:, reach_a * group : (reach_a + wide) * group] = windows

    def a_copy(k, row, target):
        lanes_of = pl.ds(pl.multiple_of(target * group, 128), cover)
        return pltpu.make_async_remote_copy(
            src_ref=wsend.at[:, lanes_of],
            dst_ref=arrived.at[row],
            send_sem=a_send.at[k - 1],
            recv_sem=a_recv.at[k - 1],
            device_id=(target, s),
            device_id_type=MESH,
        )

    for k in range(1, wide):
        a_copy(k, w, lax.rem(w + k, wide)).start()
    arrived[w] = wsend[:, pl.ds(pl.multiple_of(w * group, 128), cover)]

    mine = [nv[s * slices + z] for z in range(slices)]
    for c in range(mem):
        vol_out[c] = jnp.concatenate([m[c : c + 1] for m in mine], axis=0).astype(BF16)
    proj[...] = jnp.zeros_like(proj)
    cut[...] = jnp.zeros_like(cut)
    for i, j in d_moves:

        @pl.when(inside(w - i, s - j))
        def _():
            d_copy(i, j, (w, s)).wait_recv()

    for k in range(1, wide):
        a_copy(k, lax.rem(w + wide - k, wide), w).wait_recv()

    for a in range(wide_angles):
        at = (a - HALO + reach_a * angles) * window

        def place(g, carry):
            if groups > 1:
                select(a, g)
            halves = [arrived[g * batch + t].astype(F32)[:, at : at + window] for t in range(batch)]
            return carry + jnp.dot(
                jnp.concatenate(halves, axis=1).astype(BF16), chosen[a], preferred_element_type=F32
            )

        placed = jnp.zeros((depth, bins), F32)
        placed = place(0, placed) if groups == 1 else lax.fori_loop(0, groups, place, placed)
        scaled = (placed * (1.0 / math.sqrt(NY))).astype(BF16).astype(F32)
        for z in range(depth):
            proj[HALO + z, a : a + 1, :] = scaled[z : z + 1]

    lane = lax.broadcasted_iota(jnp.int32, (1, bins), 1)
    row8 = lax.broadcasted_iota(jnp.int32, (CH, bins), 0)
    low, high = lane > 0, lane < bins - 1
    blank = jnp.zeros((CH, bins), F32)

    def three(value):
        return (
            jnp.where(low, shifted(value, -1), 0.0),
            value,
            jnp.where(high, shifted(value, 1), 0.0),
        )

    for a in range(wide_angles):
        for z in range(deep):
            line = proj[s * slices + z, a : a + 1, :]
            value = jnp.where(row8 == 5, line, dual_in[a, z].astype(F32))
            left, mid, right = three(value)
            x1[pl.ds((a * deep + z) * 4 * CH, 4 * CH), :] = jnp.concatenate(
                [left, mid, right, blank], axis=0
            ).astype(BF16)

    def layer(weight, source, dest, out_angles, in_slices, per_slice, margin):
        out_slices = in_slices - 2
        hid = weight.shape[0] // out_slices
        rows = in_slices * per_slice
        row_z = s * slices - margin + lax.broadcasted_iota(jnp.int32, (hid * out_slices, 1), 0) // hid
        z_ok = (row_z >= 0) & (row_z < depth)
        for a in range(out_angles):
            angle = w * angles - margin + a
            ok = z_ok & (angle >= 0) & (angle < angle_total)
            value = jnp.dot(weight[...], source[pl.ds(a * rows, 3 * rows), :], preferred_element_type=F32)
            value = jnp.where(ok, jnp.maximum(value, 0.0), 0.0)
            for d2, moved in enumerate(three(value)):
                moved = moved.astype(BF16)
                for z in range(out_slices):
                    dest[pl.ds(((a * out_slices + z) * 3 + d2) * hid, hid), :] = moved[z * hid : (z + 1) * hid]

    hidden = dw2.shape[0] // (deep - 4)
    layer(dw1, x1, x2, wide_angles - 2, deep, 4 * CH, 2)
    layer(dw2, x2, x3, wide_angles - 4, deep - 2, 3 * hidden, 1)
    rows = (deep - 4) * 3 * hidden
    for a in range(angles):
        value = jnp.dot(dw3[...], x3[pl.ds(a * rows, 3 * rows), :], preferred_element_type=F32)
        own = dual_in[HALO + a, HALO : HALO + slices].astype(F32).reshape(slices * CH, bins)
        value = (own + value).astype(BF16).astype(F32)
        nd[a] = value
        for z in range(slices):
            cut[a, z : z + 1, :] = value[z * CH : z * CH + 1]

    def take(g, carry):
        found = []
        for a in range(angles):
            if groups > 1:
                select(HALO + a, g)
            found.append(
                lax.dot_general(
                    cut[a].astype(BF16), chosen[HALO + a], (((1,), (1,)), ((), ())), preferred_element_type=F32
                )
            )
        for t in range(batch):
            pieces[g * batch + t] = jnp.concatenate(
                [f[:, t * window : (t + 1) * window] for f in found], axis=1
            )
        return carry

    if groups == 1:
        take(0, 0)
    else:
        lax.fori_loop(0, groups, take, 0)

    def b_copy(k, row, target):
        return pltpu.make_async_remote_copy(
            src_ref=pieces.at[target],
            dst_ref=returned.at[row],
            send_sem=b_send.at[k - 1],
            recv_sem=b_recv.at[k - 1],
            device_id=(target, s),
            device_id_type=MESH,
        )

    for k in range(1, wide):
        b_copy(k, w, lax.rem(w + k, wide)).start()
    returned[w] = pieces[w]
    for z in range(slices):
        for c in range(mem):
            lines = [nd[a, z * CH + c : z * CH + c + 1, :] for a in range(angles)]
            dual_out[c, z] = jnp.concatenate(lines, axis=0).astype(BF16)
    for k in range(1, wide):
        b_copy(k, lax.rem(w + wide - k, wide), w).wait_recv()
    lines = jnp.concatenate([returned[t] for t in range(wide)], axis=1).astype(BF16)
    summed = lax.dot_general(lines, table[...], (((1,), (1,)), ((), ())), preferred_element_type=F32)
    back_out[...] = summed[:slices] * (1.0 / math.sqrt(angle_total))
    for k in range(1, wide):
        b_copy(k, w, lax.rem(w + k, wide)).wait_send()
    for i, j in p_moves:

        @pl.when(inside(w + i, s + j))
        def _():
            p_copy(i, j, s, (w, s)).wait_send()

    for i, j in d_moves:

        @pl.when(inside(w + i, s + j))
        def _():
            d_copy(i, j, (w, s)).wait_send()

    for k in range(1, wide):
        a_copy(k, w, lax.rem(w + k, wide)).wait_send()


def placed_band(flat, z, out_slices, block, same):
    width = flat.shape[1]
    by = ((z - 1 if same else z) * block) % width
    row = pltpu.roll(flat, by, axis=1) if by else flat
    lane = lax.broadcasted_iota(jnp.int32, (1, width), 1)
    if same and z == 0:
        row = jnp.where(lane < 2 * block, row, 0.0)
    if same and z == out_slices - 1:
        row = jnp.where(lane >= (z - 1) * block, row, 0.0)
    return row


def split_band(weights, stage, out, out_slices, same, o_pad):
    c_in, c_out = weights.shape[3:]
    block = 3 * c_in
    chunk = (out_slices if same else out_slices + 2) * block
    width = -(-chunk // 128) * 128
    held = -(-3 * block // 128) * 128
    assert width == chunk or not same
    for d1 in range(3):
        stage[...] = jnp.zeros_like(stage)
        for d0 in range(3):
            for d2 in range(3):
                at = (d0 * 3 + d2) * c_in
                stage[at : at + c_in, :c_out] = weights[d0, d1, d2].astype(F32)
        flat = stage[:held, :].T[:o_pad]
        if width > held:
            flat = jnp.concatenate([flat, jnp.zeros((o_pad, width - held), F32)], axis=1)
        for z in range(out_slices):
            row = placed_band(flat, z, out_slices, block, same)
            out[(d1 * out_slices + z) * o_pad : (d1 * out_slices + z + 1) * o_pad, :] = row[:, :chunk].astype(BF16)


def split_taps(weights, out, out_slices, same):
    c_out, _, c_in = weights.shape[2:]
    width = (out_slices if same else out_slices + 2) * c_in
    held = -(-width // 128) * 128
    assert width == held or not same
    for d1 in range(3):
        for d2 in range(3):
            lines = [weights[d0, d1, :, d2, :].astype(F32) for d0 in range(3)]
            flat = jnp.concatenate(lines + [jnp.zeros((c_out, held - 3 * c_in), F32)], axis=1)
            flat = jnp.concatenate([flat, jnp.zeros((CH - c_out, held), F32)], axis=0)
            rows = [placed_band(flat, z, out_slices, c_in, same) for z in range(out_slices)]
            at = (d1 * 3 + d2) * out_slices * CH
            out[at : at + out_slices * CH, :] = jnp.concatenate(rows, axis=0)[:, :width].astype(BF16)


def block_kernel(
    wide, slab, *refs
):
    given = refs[:12]
    vol_out, dual_out, back_out = refs[12:15]
    held, in_sem = refs[15:27], refs[27]
    volume, back_proj, dual_state, sinogram, offsets, p1, p2, p3, d1_w, d2_w, d3_w, trig = held
    (
        psrc, dsrc, frame, stack, arrived, windows, table, stage, pw1, pw2, pw3, dw1, dw2, dw3,
        px1, px2, px3, nv, dense, deck, proj, x1, x2, x3, back_out_rows, back_in, begins, wproj, xproj, base,
        p_send, p_recv, d_send, d_recv, e_send, e_recv, a_send, a_recv, b_send, b_recv,
    ) = refs[28:]
    w = lax.axis_index("wide")
    s = lax.axis_index("slab")
    mem, slices, pixels = volume.shape
    angles, bins = dual_state.shape[2:]
    angle_total = angles * wide
    depth = slices * slab
    edge = 4 * NY
    lanes = pixels + 2 * edge
    window = NY + 2 * TX
    hidden_channels = p1.shape[4]
    deep = slices + 2 * HALO
    reach_z, span_z = spans(slices)
    block = bins // wide
    broad = block + 128
    stride = block + 2 * MARGIN
    used = angle_total * stride
    total_lanes = dense.shape[1]

    def inside(i, j):
        return (i >= 0) & (i < wide) & (j >= 0) & (j < slab)

    loads = [pltpu.make_async_copy(src, dst, in_sem.at[n]) for n, (src, dst) in enumerate(zip(given, held))]
    for load in loads[:4]:
        load.start()
    frame[...] = jnp.zeros_like(frame)

    far = sorted(range(-(slab - 1), slab), key=lambda j: -abs(j))
    greet = [(i, j) for j in far for i in (0, -1, 1) if (i, j) != (0, 0)]
    barrier = pltpu.get_barrier_semaphore()
    total = jnp.int32(max(wide - 3, 0))
    for i, j in greet:
        there = inside(w + i, s + j)

        @pl.when(there)
        def _():
            pl.semaphore_signal(barrier, inc=1, device_id=(w + i, s + j), device_id_type=MESH)

        total = total + jnp.where(there, 1, 0)
    for k in range(2, wide - 1):
        pl.semaphore_signal(barrier, inc=1, device_id=(lax.rem(w + k, wide), s), device_id_type=MESH)
    if wide > 2:
        for end in (0, wide - 1):

            @pl.when(w == end)
            def _():
                pl.semaphore_signal(barrier, inc=1, device_id=(wide - 1 - end, s), device_id_type=MESH)

            total = total + jnp.where(w == end, 1, 0)

    for load in loads[:2]:
        load.wait()
    for z in range(slices):
        lines = [volume[c].astype(F32)[z : z + 1] for c in range(mem)]
        lines += [back_proj[z : z + 1, :], jnp.zeros((CH - mem - 1, pixels), F32)]
        psrc[z] = jnp.concatenate(lines, axis=0).astype(BF16)
    frame[pl.ds(s * slices, slices), :, edge : edge + pixels] = psrc[...]
    pl.semaphore_wait(barrier, total)

    def p_copy(i, j, row, target):
        if i == 0:
            src, dst = pl.ds(0, pixels), pl.ds(edge, pixels)
        elif i > 0:
            src, dst = pl.ds(pixels - edge, edge), pl.ds(0, edge)
        else:
            src, dst = pl.ds(0, edge), pl.ds(edge + pixels, edge)
        return pltpu.make_async_remote_copy(
            src_ref=psrc.at[:, :, src],
            dst_ref=frame.at[pl.ds(row * slices, slices), :, dst],
            send_sem=p_send.at[i + 1, j + slab - 1],
            recv_sem=p_recv.at[i + 1, j + slab - 1],
            device_id=target,
            device_id_type=MESH,
        )

    def d_copy(k, row, target):
        return pltpu.make_async_remote_copy(
            src_ref=dsrc.at[:, :, :, pl.ds(pl.multiple_of(target * block, 128), broad)],
            dst_ref=stack.at[pl.ds(row * angles, angles)],
            send_sem=d_send.at[k - 1],
            recv_sem=d_recv.at[k - 1],
            device_id=(target, s),
            device_id_type=MESH,
        )

    def e_copy(j, target):
        z0, zn, zd = span_z[j]
        return pltpu.make_async_remote_copy(
            src_ref=deck.at[pl.ds(HALO + z0, zn)],
            dst_ref=deck.at[pl.ds(zd, zn)],
            send_sem=e_send.at[j + reach_z],
            recv_sem=e_recv.at[j + reach_z],
            device_id=(w, target),
            device_id_type=MESH,
        )

    p_moves = greet
    e_moves = [j for j in span_z if j != 0]
    for i, j in p_moves:

        @pl.when(inside(w + i, s + j))
        def _():
            p_copy(i, j, s, (w + i, s + j)).start()

    for load in loads[2:4]:
        load.wait()
    for z in range(slices):
        for a in range(angles):
            lines = [dual_state[c, z].astype(F32)[a : a + 1] for c in range(mem)]
            lines += [jnp.zeros((1, bins), F32), sinogram[z].astype(F32)[a : a + 1]]
            lines += [jnp.zeros((CH - mem - 2, bins), F32)]
            line = jnp.concatenate([jnp.concatenate(lines, axis=0), jnp.zeros((CH, 128), F32)], axis=1)
            dsrc[a, z] = pltpu.roll(line, 64, axis=1).astype(BF16)
    for k in range(1, wide):
        d_copy(k, w, lax.rem(w + k, wide)).start()
    for load in loads[4:]:
        load.start()
    stack[pl.ds(w * angles, angles)] = dsrc[
        :, :, :, pl.ds(pl.multiple_of(w * block, 128), broad)
    ]
    dense[...] = jnp.zeros_like(dense)
    proj[...] = jnp.zeros_like(proj)
    for load in loads[4:]:
        load.wait()
    build_band(p1, stage, pw1, depth, True, CH, 4, hidden_channels)
    split_band(p2, stage, pw2, depth, True, hidden_channels)
    split_taps(p3, pw3, depth, True)
    begin_columns = offsets[...]
    for a in range(angle_total):
        begins[a] = jnp.broadcast_to(begin_columns[:, a : a + 1], (wide, 128))
    per = 128 // window
    part_of = lax.broadcasted_iota(jnp.int32, (1, 128), 1) // window
    detector = []
    for first in range(0, angle_total, per):
        own = begins[first, pl.ds(w, 1), :]
        for n in range(1, per):
            own = jnp.where(part_of == n, begins[first + n, pl.ds(w, 1), :], own)
        detector.append((lax.broadcasted_iota(jnp.int32, (1, 128), 1) - own) & (window - 1))
    build_table(trig, table, jnp.concatenate(detector, axis=1).astype(F32))
    build_band(d1_w, stage, dw1, deep - 2, False, CH, 4, hidden_channels)
    choice = lax.broadcasted_iota(jnp.int32, (1, wproj.shape[1]), 1)
    chosen_row = jnp.full_like(choice, -1)
    for d1 in range(3):
        for d2 in range(3):
            first = (d1 * 3 + d2) * deep
            here = (choice >= first) & (choice < first + deep)
            chosen_row = jnp.where(here, ((choice - first + d1 * deep) * 4 + d2) * CH + mem, chosen_row)
    picked = lax.broadcasted_iota(jnp.int32, (dw1.shape[1], wproj.shape[1]), 0) == chosen_row
    picked = jnp.where(picked, 1.0, 0.0).astype(BF16)
    wproj[...] = jnp.dot(dw1[...], picked, preferred_element_type=F32).astype(BF16)
    split_band(d2_w, stage, dw2, 2, False, hidden_channels)
    split_taps(d3_w, dw3, slices, False)
    for k in range(1, wide):
        d_copy(k, lax.rem(w + wide - k, wide), w).wait_recv()
    skip = 64 - MARGIN
    for z in range(slices):
        for a in range(angle_total):
            value = stack[a, z].astype(F32)[:, skip : skip + stride]
            dense[z * CH : (z + 1) * CH, a * stride : (a + 1) * stride] = value
        deck[HALO + z] = dense[z * CH : (z + 1) * CH, :].astype(BF16)
    for j in e_moves:

        @pl.when(inside(w, s + j))
        def _():
            e_copy(j, s + j).start()

    for i, j in p_moves:

        @pl.when(inside(w - i, s - j))
        def _():
            p_copy(i, j, s - j, (w, s)).wait_recv()


    plane = lax.broadcasted_iota(jnp.int32, (1, lanes), 1)
    y = plane % NY
    x = w * TX + plane // NY - 4
    grid_mask = (x >= 0) & (x < wide * TX)
    y_mask = {-1: y > 0, 0: None, 1: y < NY - 1}

    def tap(value, d1, d2):
        moved = shifted(value, NY * d1 + d2)
        return moved if d2 == 0 else jnp.where(y_mask[d2], moved, 0.0)

    field = frame[...].astype(F32)
    pblank = jnp.zeros((CH, lanes), F32)
    for z in range(depth):
        for d1 in range(3):
            parts = [tap(field[z], d1 - 1, d2) for d2 in (-1, 0, 1)] + [pblank]
            px1[pl.ds((d1 * depth + z) * 4 * CH, 4 * CH), :] = jnp.concatenate(parts, axis=0).astype(BF16)

    grid_top = jnp.where(grid_mask, jnp.inf, 0.0)

    def within(value):
        return jnp.minimum(jnp.maximum(value, 0.0), grid_top)

    hid = hidden_channels
    value = within(jnp.dot(pw1[...], px1[...], preferred_element_type=F32))
    for d2 in range(3):
        moved = tap(value, 0, d2 - 1).astype(BF16)
        for z in range(depth):
            px2[(z * 3 + d2) * hid : (z * 3 + d2 + 1) * hid, :] = moved[z * hid : (z + 1) * hid]
    rows = depth * hid
    value = jnp.dot(pw2[rows : 2 * rows, :], px2[...], preferred_element_type=F32)
    for d1 in (0, 2):
        part = jnp.dot(pw2[d1 * rows : (d1 + 1) * rows, :], px2[...], preferred_element_type=F32)
        value = value + shifted(part, (d1 - 1) * NY)
    px3[...] = within(value).astype(BF16)
    part = jnp.dot(pw3[...], px3[...], preferred_element_type=F32)
    rows = depth * CH
    three = jnp.zeros((rows, lanes), F32)
    for d1 in range(3):
        for d2 in range(3):
            n = d1 * 3 + d2
            three = three + tap(part[n * rows : (n + 1) * rows], d1 - 1, d2 - 1)
    updated = field.reshape(depth * CH, lanes) + three
    updated = updated[:, edge : edge + pixels].astype(BF16).astype(F32)
    nv[...] = updated.reshape(depth, CH, pixels)
    leading = jnp.concatenate([updated[z * CH : z * CH + 1] for z in range(depth)], axis=0).astype(BF16)
    windows[...] = jnp.dot(leading, table[...], preferred_element_type=F32).astype(BF16)

    def a_copy(k, row, target):
        return pltpu.make_async_remote_copy(
            src_ref=windows,
            dst_ref=arrived.at[row],
            send_sem=a_send.at[k - 1],
            recv_sem=a_recv.at[k - 1],
            device_id=(target, s),
            device_id_type=MESH,
        )

    for k in range(1, wide):
        a_copy(k, w, lax.rem(w + k, wide)).start()
    arrived[w] = windows[...]

    mine = [nv[s * slices + z] for z in range(slices)]
    for c in range(mem):
        vol_out[c] = jnp.concatenate([m[c : c + 1] for m in mine], axis=0).astype(BF16)
    for j in e_moves:

        @pl.when(inside(w, s - j))
        def _():
            e_copy(j, s).wait_recv()

    lane = lax.broadcasted_iota(jnp.int32, (1, total_lanes), 1)
    begin = jnp.zeros_like(lane)
    for a in range(1, angle_total):
        begin = jnp.where(lane >= a * stride, a * stride, begin)
    bin_at = w * block - MARGIN + lane - begin
    lane_top = jnp.where((lane < used) & (bin_at >= 0) & (bin_at < bins), jnp.inf, 0.0)
    blank = jnp.zeros((CH, total_lanes), F32)
    for z in range(deep):
        value = deck[z].astype(F32)
        if z < HALO or z >= HALO + slices:
            row_z = s * slices + z - HALO
            value = jnp.where((row_z >= 0) & (row_z < depth), value, 0.0)
        for d1 in range(3):
            parts = [shifted(value, (d1 - 1) * stride + d2 - 1) for d2 in range(3)] + [blank]
            x1[(d1 * deep + z) * 4 * CH : (d1 * deep + z + 1) * 4 * CH, :] = jnp.concatenate(parts, axis=0).astype(BF16)
    base[...] = jnp.dot(dw1[...], x1[...], preferred_element_type=F32)
    for k in range(1, wide):
        a_copy(k, lax.rem(w + wide - k, wide), w).wait_recv()

    at = lax.broadcasted_iota(jnp.int32, (depth, 128), 1)
    bins_at = [at + (w * block - 64 + n * 128) for n in range(broad // 128)]
    for first in range(0, angle_total, per):
        placed = [[jnp.zeros((depth, 128), F32) for _ in bins_at] for _ in range(per)]
        for t in range(wide):
            source = arrived[t, :, first * window : first * window + 128].astype(F32)
            for n in range(per):
                line = source
                for m in range(per):
                    if m != n:
                        line = jnp.where(at // window == m, pltpu.roll(source, (m - n) * window % 128, axis=1), line)
                begin = begins[first + n, t : t + 1, :]
                for m, bin_of in enumerate(bins_at):
                    inner = bin_of - begin
                    placed[n][m] = placed[n][m] + jnp.where((inner >= 0) & (inner < window), line, 0.0)
        for n in range(per):
            line = jnp.concatenate(placed[n], axis=1) * (1.0 / math.sqrt(NY))
            line = line.astype(BF16).astype(F32)[:, skip : skip + stride]
            proj[8 : 8 + depth, (first + n) * stride : (first + n + 1) * stride] = line

    def kept(value, out_slices, margin):
        hid = value.shape[0] // out_slices
        parts = []
        for z in range(out_slices):
            row_z = s * slices - margin + z
            top = jnp.where((row_z >= 0) & (row_z < depth), lane_top, 0.0)
            parts.append(jnp.minimum(jnp.maximum(value[z * hid : (z + 1) * hid], 0.0), top))
        return jnp.concatenate(parts, axis=0)

    line = jnp.concatenate([proj[pl.ds(8 - HALO + s * slices + z, 1), :] for z in range(deep)], axis=0)
    parts = [shifted(line, (d1 - 1) * stride + d2 - 1) for d1 in range(3) for d2 in range(3)]
    parts += [jnp.zeros((xproj.shape[0] - 9 * deep, total_lanes), F32)]
    xproj[...] = jnp.concatenate(parts, axis=0).astype(BF16)
    hid = hidden_channels
    value = base[...] + jnp.dot(wproj[...], xproj[...], preferred_element_type=F32)
    value = kept(value, deep - 2, 2)
    for d2 in range(3):
        moved = shifted(value, d2 - 1).astype(BF16)
        for z in range(deep - 2):
            x2[(z * 3 + d2) * hid : (z * 3 + d2 + 1) * hid, :] = moved[z * hid : (z + 1) * hid]
    rows = 2 * hid
    for z in range(0, deep - 4, 2):
        source = x2[z * 3 * hid : (z + 4) * 3 * hid, :]
        part = jnp.dot(dw2[...], source, preferred_element_type=F32)
        value = part[rows : 2 * rows]
        for d1 in (0, 2):
            value = value + shifted(part[d1 * rows : (d1 + 1) * rows], (d1 - 1) * stride)
        x3[z * hid : (z + 2) * hid, :] = kept(value, 2, 1 - z).astype(BF16)
    part = jnp.dot(dw3[...], x3[...], preferred_element_type=F32)
    rows = slices * CH
    value = dense[...]
    for d1 in range(3):
        for d2 in range(3):
            n = d1 * 3 + d2
            value = value + shifted(part[n * rows : (n + 1) * rows], (d1 - 1) * stride + d2 - 1)
    value = value.astype(BF16).astype(F32)
    heads = []
    for a in range(angle_total):
        own = value[:, a * stride + MARGIN : a * stride + MARGIN + block]
        owner, at_row = a // angles, a % angles * rows
        back_out_rows[owner, at_row : at_row + rows, :] = own.astype(BF16)
        heads += [own[z * CH : z * CH + 1] for z in range(slices)]
    heads = jnp.concatenate(heads, axis=0).astype(BF16)
    for t in range(wide):
        back_out_rows[t, angles * rows :, :] = heads

    def b_copy(k, row, target):
        return pltpu.make_async_remote_copy(
            src_ref=back_out_rows.at[target],
            dst_ref=back_in.at[:, pl.ds(pl.multiple_of(row * block, 128), block)],
            send_sem=b_send.at[k - 1],
            recv_sem=b_recv.at[k - 1],
            device_id=(target, s),
            device_id_type=MESH,
        )

    for k in range(1, wide):
        b_copy(k, w, lax.rem(w + k, wide)).start()
    back_in[:, pl.ds(pl.multiple_of(w * block, 128), block)] = back_out_rows[w]
    for i, j in p_moves:

        @pl.when(inside(w + i, s + j))
        def _():
            p_copy(i, j, s, (w, s)).wait_send()

    for k in range(1, wide):
        d_copy(k, w, lax.rem(w + k, wide)).wait_send()
    for j in e_moves:

        @pl.when(inside(w, s + j))
        def _():
            e_copy(j, s + j).wait_send()

    for k in range(1, wide):
        a_copy(k, w, lax.rem(w + k, wide)).wait_send()
    for k in range(1, wide):
        b_copy(k, w, lax.rem(w + k, wide)).wait_send()
    for k in range(1, wide):
        b_copy(k, lax.rem(w + wide - k, wide), w).wait_recv()
    line8 = lax.broadcasted_iota(jnp.int32, (8, 128), 0)
    lane8 = lax.broadcasted_iota(jnp.int32, (8, 128), 1)
    cut = back_in[angles * rows :, :].astype(F32)
    taken = []
    for first in range(0, angle_total, per):
        joined = jnp.zeros((8, 128), F32)
        for n in range(per):
            a = first + n
            begin = begins[a, pl.ds(w, 1), :]
            group = a * slices // 8 * 8
            found = jnp.zeros((8, 128), F32)
            for m in range(0, bins, 128):
                inner = lane8 + m - begin
                found = jnp.where((inner >= 0) & (inner < window), cut[group : group + 8, m : m + 128], found)
            both = found
            for m in range(1, per):
                both = both + pltpu.roll(found, m * window, axis=1)
            at_row = a * slices - group
            here = (lane8 // window == n) & (line8 >= at_row) & (line8 < at_row + slices)
            joined = jnp.where(here, both, joined)
        taken.append(joined)
    lines = jnp.concatenate(taken, axis=1).astype(BF16)
    summed = lax.dot_general(lines, table[...], (((1,), (1,)), ((), ())), preferred_element_type=F32)
    total_back = summed[:slices]
    for n in range(1, 8 // slices):
        total_back = total_back + summed[n * slices : (n + 1) * slices]
    back_out[...] = total_back * (1.0 / math.sqrt(angle_total))
    mine = back_in[: angles * rows, :].astype(F32)
    for z in range(slices):
        for c in range(mem):
            at_rows = [a * rows + z * CH + c for a in range(angles)]
            lines = [mine[n : n + 1] for n in at_rows]
            dual_out[c, z] = jnp.concatenate(lines, axis=0).astype(BF16)


def hand_on(outs):
    def kernel(*refs):
        for src, dst in zip(refs[:3], refs[3:]):
            dst[...] = src[...]

    space = pl.BlockSpec(memory_space=pltpu.VMEM)
    return pl.pallas_call(
        kernel,
        out_shape=tuple(jax.ShapeDtypeStruct(o.shape, o.dtype) for o in outs),
        in_specs=[space] * 3,
        out_specs=(space,) * 3,
        name="hand_on",
    )(*outs)


def block_body(wide, slab, volume, back_proj, dual_state, sinogram, offsets, p1, p2, p3, d1, d2, d3):
    mem, slices, pixels = volume.shape
    angles, bins = dual_state.shape[2:]
    depth = slices * slab
    angle_total = angles * wide
    hidden = p1.shape[4]
    reach_z, _ = spans(slices)
    lanes = pixels + 8 * NY
    window = NY + 2 * TX
    block = bins // wide
    stride = block + 2 * MARGIN
    spread_lanes = -(-((angle_total + 1) * stride + 1) // 128) * 128
    deep = slices + 2 * HALO
    dma = pltpu.SemaphoreType.DMA
    vmem = pltpu.VMEM
    space = pl.BlockSpec(memory_space=pltpu.VMEM)
    args = (volume, back_proj, dual_state, sinogram, offsets, p1, p2, p3.transpose(0, 1, 4, 2, 3))
    args += (d1, d2, d3.transpose(0, 1, 4, 2, 3), jnp.asarray(trig_rows(angle_total)))
    outs = pl.pallas_call(
        functools.partial(block_kernel, wide, slab),
        out_shape=(
            jax.ShapeDtypeStruct(volume.shape, BF16),
            jax.ShapeDtypeStruct(dual_state.shape, BF16),
            jax.ShapeDtypeStruct(back_proj.shape, F32),
        ),
        in_specs=[pl.BlockSpec(memory_space=pl.ANY)] * 12,
        out_specs=(space,) * 3,
        scratch_shapes=[vmem(a.shape, a.dtype) for a in args]
        + [dma((12,))]
        + [
            vmem((slices, CH, pixels), BF16),
            vmem((angles, slices, CH, bins + 128), BF16),
            vmem((depth, CH, lanes), BF16),
            vmem((angle_total, slices, CH, block + 128), BF16),
            vmem((wide, depth, angle_total * window), BF16),
            vmem((depth, angle_total * window), BF16),
            vmem((pixels, angle_total * window), BF16),
            vmem((-(-9 * hidden // 128) * 128, 128), F32),
            vmem((depth * hidden, 12 * depth * CH), BF16),
            vmem((3 * depth * hidden, 3 * depth * hidden), BF16),
            vmem((9 * depth * CH, depth * hidden), BF16),
            vmem(((deep - 2) * hidden, 12 * deep * CH), BF16),
            vmem((6 * hidden, 12 * hidden), BF16),
            vmem((9 * slices * CH, (deep - 4) * hidden), BF16),
            vmem((12 * depth * CH, lanes), BF16),
            vmem((3 * depth * hidden, lanes), BF16),
            vmem((depth * hidden, lanes), BF16),
            vmem((depth, CH, pixels), F32),
            vmem((slices * CH, spread_lanes), F32),
            vmem((deep, CH, spread_lanes), BF16),
            vmem((-(-depth // 8) * 8 + 16, spread_lanes), F32),
            vmem((12 * deep * CH, spread_lanes), BF16),
            vmem((3 * (deep - 2) * hidden, spread_lanes), BF16),
            vmem(((deep - 4) * hidden, spread_lanes), BF16),
            vmem((wide, (angles * CH + angle_total) * slices, block), BF16),
            vmem(((angles * CH + angle_total) * slices, bins), BF16),
            vmem((angle_total, wide, 128), jnp.int32),
            vmem(((deep - 2) * hidden, -(-9 * deep // 16) * 16), BF16),
            vmem((-(-9 * deep // 16) * 16, spread_lanes), BF16),
            vmem(((deep - 2) * hidden, spread_lanes), F32),
            dma((3, 2 * slab - 1)),
            dma((3, 2 * slab - 1)),
            dma((wide - 1,)),
            dma((wide - 1,)),
            dma((2 * reach_z + 1,)),
            dma((2 * reach_z + 1,)),
            dma((wide - 1,)),
            dma((wide - 1,)),
            dma((wide - 1,)),
            dma((wide - 1,)),
        ],
        compiler_params=pltpu.CompilerParams(
            collective_id=0, has_side_effects=True, vmem_limit_bytes=VMEM_LIMIT
        ),
        name="block_kernel",
    )(*args)
    return hand_on(outs)


def body(wide, slab, volume, back_proj, dual_state, sinogram, offsets, p1, p2, p3, d1, d2, d3):
    mem, slices, pixels = volume.shape
    angles, bins = dual_state.shape[2:]
    if bins % (128 * wide) == 0 and 8 % slices == 0 and (slices + 2 * HALO) % 8 == 0 and angles * wide * slices % 16 == 0:
        return block_body(wide, slab, volume, back_proj, dual_state, sinogram, offsets, p1, p2, p3, d1, d2, d3)
    depth = slices * slab
    angle_total = angles * wide
    hidden = p1.shape[4]
    group = angles * (NY + 2 * TX)
    reach_a, _ = spans(angles)
    reach_z, _ = spans(slices)
    lanes = pixels + 8 * NY
    wide_angles = angles + 2 * HALO
    deep = slices + 2 * HALO
    dma = pltpu.SemaphoreType.DMA
    vmem = pltpu.VMEM
    space = pl.BlockSpec(memory_space=pltpu.VMEM)
    args = (volume, back_proj, dual_state, sinogram, offsets, p1, p2, p3.transpose(0, 1, 4, 2, 3))
    args += (d1, d2, d3.transpose(0, 1, 4, 2, 3), jnp.asarray(trig_rows(angle_total)))
    outs = pl.pallas_call(
        functools.partial(whole_kernel, wide, slab),
        out_shape=(
            jax.ShapeDtypeStruct(volume.shape, BF16),
            jax.ShapeDtypeStruct(dual_state.shape, BF16),
            jax.ShapeDtypeStruct(back_proj.shape, F32),
        ),
        in_specs=[pl.BlockSpec(memory_space=pl.ANY)] * 12,
        out_specs=(space,) * 3,
        scratch_shapes=[vmem(a.shape, a.dtype) for a in args]
        + [dma((12,))]
        + [
            vmem((slices, CH, pixels), BF16),
            vmem((angles, slices, CH, bins), BF16),
            vmem((depth, CH, lanes), BF16),
            vmem((wide_angles, deep, CH, bins), BF16),
            vmem((wide, depth, (2 * reach_a + 1) * group), BF16),
            vmem((depth, (wide + 2 * reach_a) * group), BF16),
            vmem((pixels, angle_total * (NY + 2 * TX)), BF16),
            vmem((-(-9 * hidden // 128) * 128, 128), F32),
            vmem((depth * hidden, 12 * depth * CH), BF16),
            vmem((depth * hidden, 9 * depth * hidden), BF16),
            vmem((depth * CH, 9 * depth * hidden), BF16),
            vmem(((deep - 2) * hidden, 12 * deep * CH), BF16),
            vmem(((deep - 4) * hidden, 9 * (deep - 2) * hidden), BF16),
            vmem(((deep - 6) * CH, 9 * (deep - 4) * hidden), BF16),
            vmem((12 * depth * CH, lanes), BF16),
            vmem((9 * depth * hidden, lanes), BF16),
            vmem((depth, CH, pixels), F32),
            vmem((wide_angles, math.gcd(wide, 8) * (NY + 2 * TX), bins), BF16),
            vmem((depth + 2 * HALO, wide_angles, bins), F32),
            vmem((wide_angles * deep * 4 * CH, bins), BF16),
            vmem(((wide_angles - 2) * (deep - 2) * 3 * hidden, bins), BF16),
            vmem(((wide_angles - 4) * (deep - 4) * 3 * hidden, bins), BF16),
            vmem((angles, slices * CH, bins), F32),
            vmem((angles, 8, bins), F32),
            vmem((wide, 8, group), F32),
            vmem((wide, 8, group), F32),
            dma((3, 2 * slab - 1)),
            dma((3, 2 * slab - 1)),
            dma((2 * reach_a + 1, 2 * reach_z + 1)),
            dma((2 * reach_a + 1, 2 * reach_z + 1)),
            dma((wide - 1,)),
            dma((wide - 1,)),
            dma((wide - 1,)),
            dma((wide - 1,)),
        ],
        compiler_params=pltpu.CompilerParams(
            collective_id=0, has_side_effects=True, vmem_limit_bytes=VMEM_LIMIT
        ),
        name="whole_kernel",
    )(*args)
    return hand_on(outs)


def solution(mesh):
    wide, slab = mesh.shape["wide"], mesh.shape["slab"]
    in_specs = (
        P(None, "slab", "wide"),
        P("slab", "wide"),
        P(None, "slab", "wide", None),
        P("slab", "wide", None),
    ) + (P(),) * 7
    out_specs = (P(None, "slab", "wide"), P(None, "slab", "wide", None), P("slab", "wide"))
    return jax.shard_map(
        functools.partial(body, wide, slab), mesh=mesh, in_specs=in_specs, out_specs=out_specs, check_vma=False
    )
```
